128 devices in a mesh: dp: 32 (over z_hi, y, x), mp: 4 (over z_lo, core).
Axes of the slice: x: 4, y: 4, z: 4 (z_hi: 2, z_lo: 2; z = z_hi * 2 + z_lo), core: 2. Of those that a mesh axis runs over, the one named last changes fastest.
Arguments:
- gradients: bfloat16 [32, 40, 512, 512], P('dp', 'mp'), may hold values from -16 to 16
- factor_state: float32 [4, 32, 2, 2, 512, 512], P('mp', 'dp'), as said below
- block_owner: int32 [4, 10], P('mp'), may hold values from 0 to 31, as said below
Outputs:
- directions: bfloat16 [40, 512, 512], P('mp')
- next_state: float32 [4, 32, 2, 2, 512, 512], P('mp', 'dp')
The draws below stay inside these ranges and needn't reach their ends.
Inputs may be any that keep to these rules, and one draw needn't show every extreme that they name: `block_owner`: within one row (one index of mp) no owner appears more than 2 times, and some owner appears exactly 2 times. Every index of dp owns some block. `factor_state`: every factor matrix is symmetric positive definite.
All inputs are finite; a program needn't handle non-finite values.
Results may differ from the reference program's by a relative error of at most 0.0004.
Values may be sent and summed in bfloat16 or wider, within the bound.
No kernel may reach another device: no remote copies, remote signals or barrier semaphores. Data moves between devices by JAX's collectives and lax.ppermute only.
A program may use at most 128 MiB of HBM per device.

```python
import jax
import jax.numpy as jnp
from jax import lax

BS = 512
BLK_MP = 10
SLOTS = 2
ITERS = 3
BLOCKS = 40
N_DP = 32
N_MP = 4


def draw_gradients(key, part):
    subkeys = jax.random.split(key, 3)
    positions = jnp.arange(BLOCKS, dtype=jnp.float32) / max(BLOCKS - 1, 1)
    row_scale = jnp.exp(jax.random.uniform(subkeys[0], (BLOCKS, BS), jnp.float32, -0.6931, 0.6931))
    column_scale = jnp.exp(jax.random.uniform(subkeys[1], (BLOCKS, BS), jnp.float32, -0.6931, 0.6931))
    array_shape = (N_DP, BLOCKS, BS, BS)
    noise = jax.random.normal(subkeys[2], array_shape, jnp.float32)
    block_scale = 4.0 ** positions
    values = 0.2 * noise * block_scale[None, :, None, None] * row_scale[None, :, :, None] * column_scale[None, :, None, :]
    return jnp.clip(values, -16.0, 16.0).astype(jnp.bfloat16)


def draw_factor_state(key, part):
    first, second = jax.random.split(key)
    array_shape = (N_MP, N_DP, SLOTS, 2, BS, BS)
    basis = jax.random.normal(first, array_shape, jnp.float32)
    weights = jnp.exp(jax.random.uniform(second, array_shape[:-1], jnp.float32, -0.6931, 1.3863))
    gram = jnp.einsum('abcdik,abcdjk->abcdij', basis, basis) * (2.0 / BS)
    return gram + weights[..., None] * jnp.eye(BS, dtype=jnp.float32)


def owner_row(key, ranking, row_index):
    start = row_index * (BLK_MP - 1)
    steps = jnp.arange(BLK_MP, dtype=jnp.int32)
    if BLK_MP > N_DP:
        picks = (start + steps) % N_DP
    else:
        picks = (start + jnp.where(steps == BLK_MP - 1, 0, steps)) % N_DP
    listed = ranking[picks].astype(jnp.int32)
    arrangement = jax.random.permutation(key, BLK_MP)
    return listed[arrangement]


def draw_block_owner(key, part):
    ranking = jax.random.permutation(jax.random.fold_in(key, 7001), N_DP).astype(jnp.int32)
    rows = [owner_row(jax.random.fold_in(key, row_index), ranking, row_index) for row_index in range(N_MP)]
    return jnp.stack(rows)


def setup_inputs(seed: int = 0) -> dict:
    splits = jax.random.split(jax.random.key(seed), 4)
    gradients = draw_gradients(jax.random.fold_in(splits[3], 71), 0)
    factor_state = draw_factor_state(jax.random.fold_in(splits[3], 71), 0)
    block_owner = draw_block_owner(jax.random.fold_in(splits[3], 71), 0)
    return dict(gradients=gradients, factor_state=factor_state, block_owner=block_owner)


decay_rate = 0.95
ridge_term = 0.001
tiny_offset = 1e-06

def product(left, right):
    return jnp.dot(left, right, precision=lax.Precision.HIGHEST)

def inverse_root(matrix):
    width_rows = matrix.shape[0]
    identity = jnp.eye(width_rows, dtype=matrix.dtype)
    shifted = matrix + ridge_term * identity
    level_norm = jnp.sqrt(jnp.sum(shifted * shifted))
    moving = shifted / level_norm
    result = identity * level_norm ** (-0.25)
    for turn_index in range(ITERS):
        factor = (5.0 * identity - moving) * 0.25
        result = product(result, factor)
        if turn_index + 1 < ITERS:
            square = product(factor, factor)
            fourth = product(square, square)
            moving = product(fourth, moving)
    return result

def grafted(gradient, left_root, right_root):
    precond = product(product(left_root, gradient), right_root)
    target = jnp.sqrt(jnp.mean(gradient * gradient) + tiny_offset)
    actual = jnp.sqrt(jnp.mean(precond * precond) + tiny_offset)
    return precond * (target / actual)

def owner_slots(owners):
    block_count = owners.shape[0]
    positions = jnp.arange(block_count, dtype=jnp.int32)
    same_owner = owners[:, None] == owners[None, :]
    earlier = positions[None, :] < positions[:, None]
    return lax.optimization_barrier(jnp.sum((same_owner & earlier).astype(jnp.int32), axis=1))

def reference(gradients, factor_state, block_owner):

    def accumulate(replica, running):
        return running + gradients[replica].astype(running.dtype)
    summed = lax.fori_loop(0, gradients.shape[0], accumulate, jnp.zeros(gradients.shape[1:], jnp.float32))
    clip_value = 1.0 / jnp.sqrt(jnp.mean(summed * summed) + tiny_offset)
    clipped = summed * clip_value
    mp_index = jnp.arange(BLOCKS, dtype=jnp.int32) // BLK_MP
    owners = block_owner.reshape(-1).astype(jnp.int32)
    slot_of = jax.vmap(owner_slots)(block_owner).reshape(-1).astype(jnp.int32)
    old_pairs = factor_state[mp_index, owners, slot_of]

    def one_block(items):
        gradient, old_pair = items
        left = decay_rate * old_pair[0] + (1.0 - decay_rate) * product(gradient, gradient.T)
        right = decay_rate * old_pair[1] + (1.0 - decay_rate) * product(gradient.T, gradient)
        direction = grafted(gradient, inverse_root(left), inverse_root(right)).astype(jnp.bfloat16)
        return (direction, jnp.stack([left, right]))
    directions, pairs = lax.map(one_block, (clipped, old_pairs))
    next_state = factor_state.at[mp_index, owners, slot_of].set(pairs)
    return (directions, next_state)
```

```python
import jax
import jax.numpy as jnp
from jax import lax
from jax.experimental import pallas as pl
from jax.experimental.pallas import tpu as pltpu
from jax.sharding import PartitionSpec as P

SLOTS = 2
N = 512
BLK = 10
NDP = 32
PIECE = N // NDP
HALF = BLK // 2
TR = 256
F32 = jnp.float32
BF = jnp.bfloat16

decay_rate = 0.95
ridge_term = 0.001
tiny_offset = 1e-06


def dp_pairs(dx, dy, dz):
    pairs = []
    for z in range(2):
        for y in range(4):
            for x in range(4):
                to = ((z + dz) % 2) * 16 + ((y + dy) % 4) * 4 + (x + dx) % 4
                pairs.append((z * 16 + y * 4 + x, to))
    return pairs


CORE_PAIRS = [(0, 1), (1, 0), (2, 3), (3, 2)]


def split(v):
    hi = v.astype(BF)
    return hi, (v - hi.astype(F32)).astype(BF)


def dot(a, b):
    return jnp.dot(a, b, preferred_element_type=F32)


def on_diagonal(r):
    i = lax.broadcasted_iota(jnp.int32, (TR, N), 0) + r * TR
    j = lax.broadcasted_iota(jnp.int32, (TR, N), 1)
    return i == j


def store(ref, rows, v):
    hi, lo = split(v)
    ref[0, rows, :] = hi
    ref[1, rows, :] = lo


def product(a, b, finish):
    for r in range(N // TR):
        rows = pl.ds(r * TR, TR)
        ah = a[0, rows, :]
        al = a[1, rows, :]
        finish(r, rows, dot(ah, b[0]) + (dot(ah, b[1]) + dot(al, b[0])))


def power_eighth(total):
    wide = jnp.full((8, 128), total, F32)
    return (1.0 / jnp.sqrt(jnp.sqrt(jnp.sqrt(wide))))[0:1, 0:1]


def reduce_kernel(index_ref, recv_ref, out_ref, square_ref, total, squares):
    b = pl.program_id(0)
    value = recv_ref[0, 0].astype(F32)
    for r in range(1, NDP):
        value += recv_ref[r, 0].astype(F32)
    total[b] = value

    @pl.when(b == 0)
    def _():
        squares[...] = jnp.zeros_like(squares)

    squares[...] += value * value

    @pl.when(b == BLK - 1)
    def _():
        square_ref[...] = jnp.broadcast_to(jnp.sum(squares[...]), square_ref.shape)
        for s in range(SLOTS):

            @pl.loop(0, NDP)
            def _(o):
                out_ref[o, s] = total[index_ref[s, o]]


def reduce_pack(index, recv):
    return pl.pallas_call(
        reduce_kernel,
        grid=(BLK,),
        in_specs=[
            pl.BlockSpec(memory_space=pltpu.SMEM),
            pl.BlockSpec((NDP, 1, PIECE, N), lambda b: (0, b, 0, 0)),
        ],
        out_specs=[
            pl.BlockSpec((NDP, SLOTS, PIECE, N), lambda b: (0, 0, 0, 0)),
            pl.BlockSpec((8, 128), lambda b: (0, 0)),
        ],
        out_shape=[
            jax.ShapeDtypeStruct((NDP, SLOTS, PIECE, N), F32),
            jax.ShapeDtypeStruct((8, 128), F32),
        ],
        scratch_shapes=[pltpu.VMEM((BLK, PIECE, N), F32), pltpu.VMEM((PIECE, N), F32)],
        compiler_params=pltpu.CompilerParams(dimension_semantics=("arbitrary",)),
        cost_estimate=pl.CostEstimate(flops=5_000_000, bytes_accessed=7_500_000, transcendentals=0),
        name="reduce_pack",
    )(index, recv)


def task_kernel(occ, clip, g_ref, old_ref, dir_ref, g2, gt2, full, m, f, p, q, m1, f1, x2, u, norms):
    @pl.when(occ[0] > 0)
    def _():
        g = g_ref[...].reshape(N, N) * clip[0]
        squares = jnp.sum(g * g)
        store(g2, pl.ds(0, N), g)
        store(gt2, pl.ds(0, N), g.T)

        def root(side, carry):
            def gram(a, b):
                def finish(r, rows, acc):
                    mixed = decay_rate * old_ref[0, 0, 0, side, rows, :] + (1.0 - decay_rate) * acc
                    full[rows, :] = mixed + jnp.where(on_diagonal(r), ridge_term, 0.0)

                product(a, b, finish)

            @pl.when(side == 0)
            def _():
                gram(g2, gt2)

            @pl.when(side == 1)
            def _():
                gram(gt2, g2)

            whole = full[...]
            norm2 = jnp.sum(whole * whole)
            norms[side] = norm2
            inverse = (1.0 / jnp.sqrt(jnp.full((8, 128), norm2, F32)))[0:1, 0:1]

            def factor(r, moving):
                return jnp.where(on_diagonal(r), 1.25, 0.0) - 0.25 * moving

            def halves_to(ref):
                return lambda r, rows, acc: store(ref, rows, acc)

            for r in range(N // TR):
                rows = pl.ds(r * TR, TR)
                moving = full[rows, :] * inverse
                store(m, rows, moving)
                store(f, rows, factor(r, moving))

            def first(r, rows, acc):
                store(m1, rows, acc)
                store(f1, rows, factor(r, acc))

            product(f, f, halves_to(p))
            product(p, p, halves_to(q))
            product(q, m, first)
            product(f, f1, halves_to(x2))
            product(f1, f1, halves_to(p))
            product(p, p, halves_to(q))
            product(q, m1, lambda r, rows, acc: store(m, rows, factor(r, acc)))
            product(x2, m, halves_to(u.at[side]))
            return carry

        lax.fori_loop(0, 2, root, 0)

        def last(r, rows, acc):
            full[rows, :] = acc

        product(u.at[0], g2, lambda r, rows, acc: store(p, rows, acc))
        product(p, u.at[1], last)
        precond = full[...] * (power_eighth(norms[0]) * power_eighth(norms[1]))
        entries = N * N
        actual = jnp.full((8, 128), jnp.sum(precond * precond) / entries + tiny_offset, F32)
        target = jnp.full((8, 128), squares / entries + tiny_offset, F32)
        graft = (jnp.sqrt(target) / jnp.sqrt(actual))[0:1, 0:1]
        dir_ref[...] = (precond * graft).astype(BF).reshape(dir_ref.shape)

    @pl.when(occ[0] <= 0)
    def _():
        dir_ref[...] = jnp.zeros_like(dir_ref)


def pair():
    return pltpu.VMEM((2, N, N), BF)


def run_task(occupied, clip, gathered, pairs, slot):
    return pl.pallas_call(
        task_kernel,
        grid=(1,),
        in_specs=[
            pl.BlockSpec(memory_space=pltpu.SMEM),
            pl.BlockSpec(memory_space=pltpu.SMEM),
            pl.BlockSpec((NDP, 1, PIECE, N), lambda i: (0, slot if gathered.shape[1] > 1 else 0, 0, 0)),
            pl.BlockSpec((1, 1, 1, 2, N, N), lambda i: (0, 0, slot if pairs.shape[2] > 1 else 0, 0, 0, 0)),
        ],
        out_specs=pl.BlockSpec((NDP, 1, PIECE, N), lambda i: (0, 0, 0, 0)),
        out_shape=jax.ShapeDtypeStruct((NDP, 1, PIECE, N), BF),
        scratch_shapes=[pair(), pair(), pltpu.VMEM((N, N), F32)]
        + [pair() for _ in range(7)]
        + [pltpu.VMEM((2, 2, N, N), BF), pltpu.SMEM((2,), F32)],
        compiler_params=pltpu.CompilerParams(vmem_limit_bytes=40 << 20),
        cost_estimate=pl.CostEstimate(flops=16_000_000_000, bytes_accessed=3_500_000, transcendentals=0),
        name=f"task{slot}",
    )(occupied, clip, gathered, pairs)


def state_kernel(occ, clip, g_ref, old_ref, new_ref, g2, gt2):
    s = pl.program_id(0)

    @pl.when(occ[s] > 0)
    def _():
        g = g_ref[...].reshape(N, N) * clip[0]
        store(g2, pl.ds(0, N), g)
        store(gt2, pl.ds(0, N), g.T)

        def mix(side):
            def finish(r, rows, acc):
                new_ref[0, 0, 0, side, rows, :] = (
                    decay_rate * old_ref[0, 0, 0, side, rows, :] + (1.0 - decay_rate) * acc
                )

            return finish

        product(g2, gt2, mix(0))
        product(gt2, g2, mix(1))

    @pl.when(occ[s] <= 0)
    def _():
        new_ref[...] = old_ref[...]


def new_state(occupied, clip, gathered, pairs):
    block = pl.BlockSpec((1, 1, 1, 2, N, N), lambda s: (0, 0, s, 0, 0, 0))
    return pl.pallas_call(
        state_kernel,
        grid=(SLOTS,),
        in_specs=[
            pl.BlockSpec(memory_space=pltpu.SMEM),
            pl.BlockSpec(memory_space=pltpu.SMEM),
            pl.BlockSpec((NDP, 1, PIECE, N), lambda s: (0, s, 0, 0)),
            block,
        ],
        out_specs=block,
        out_shape=jax.ShapeDtypeStruct(pairs.shape, F32),
        scratch_shapes=[pair(), pair()],
        compiler_params=pltpu.CompilerParams(dimension_semantics=("arbitrary",)),
        cost_estimate=pl.CostEstimate(flops=3_000_000_000, bytes_accessed=10_000_000, transcendentals=0),
        name="state",
    )(occupied, clip, gathered, pairs)


def pick_kernel(owner, slot, recv_ref, out_ref):
    for b in range(BLK):
        out_ref[b] = recv_ref[owner[b], slot[b]]


def pick(owner, slot, recv):
    return pl.pallas_call(
        pick_kernel,
        in_specs=[pl.BlockSpec(memory_space=pltpu.SMEM)] * 2 + [pl.BlockSpec(memory_space=pltpu.VMEM)],
        out_specs=pl.BlockSpec(memory_space=pltpu.VMEM),
        out_shape=jax.ShapeDtypeStruct((BLK, PIECE, N), BF),
        name="pick",
    )(owner, slot, recv)


def place_kernel(place, *refs):
    first, second, out, sems = refs[:4], refs[4:8], refs[8], refs[9]
    x, y, z = place[0], place[1], place[2]
    copies = []
    for far in range(4):
        for near in range(4):
            for dz in range(2):
                for group, dx, dy, ref in ((0, far, near, first[far]), (1, near, far, second[far])):
                    source = lax.rem(z + dz, 2) * 16 + lax.rem(y + 4 - dy, 4) * 4 + lax.rem(x + 4 - dx, 4)
                    row = pl.multiple_of(source * PIECE, PIECE)
                    copies.append(
                        pltpu.make_async_copy(
                            ref.at[near, dz],
                            out.at[pl.ds(group * HALF, HALF), pl.ds(row, PIECE), :],
                            sems.at[len(copies)],
                        )
                    )
    for copy in copies:
        copy.start()
    for copy in copies:
        copy.wait()


def place_all(place, first, second):
    return pl.pallas_call(
        place_kernel,
        in_specs=[pl.BlockSpec(memory_space=pltpu.SMEM)] + [pl.BlockSpec(memory_space=pltpu.VMEM)] * 8,
        out_specs=pl.BlockSpec(memory_space=pl.ANY),
        out_shape=jax.ShapeDtypeStruct((BLK, N, N), BF),
        scratch_shapes=[pltpu.SemaphoreType.DMA((64,))],
        name="place",
    )(place, *first, *second)


def spread(v, dx, dy, dz):
    steps = 2 if dz else 4
    return [v] + [lax.ppermute(v, "dp", dp_pairs(dx * k, dy * k, dz * k)) for k in range(1, steps)]


def owner_slots(owners):
    positions = jnp.arange(owners.shape[0], dtype=jnp.int32)
    same_owner = owners[:, None] == owners[None, :]
    earlier = positions[None, :] < positions[:, None]
    return jnp.sum((same_owner & earlier).astype(jnp.int32), axis=1)


def shards(gradients, factor_state, block_owner):
    owners = block_owner[0]
    myself = lax.axis_index("dp")
    slot_of = owner_slots(owners)
    positions = jnp.arange(BLK, dtype=jnp.int32)
    slots = jnp.arange(SLOTS, dtype=jnp.int32)
    devices = jnp.arange(NDP, dtype=jnp.int32)
    match = (owners == devices[None, :, None]) & (slot_of == slots[:, None, None])
    index = jnp.sum(jnp.where(match, positions, 0), axis=2)
    mine = (owners == myself) & (slot_of == slots[:, None])
    occupied = jnp.max(mine.astype(jnp.int32), axis=1)
    other_occupied = lax.ppermute(occupied[1:2], "mp", CORE_PAIRS)
    other_pair = lax.ppermute(factor_state[:, :, 1:2], "mp", CORE_PAIRS)

    pieces = gradients[0].reshape(BLK, NDP, PIECE, N)
    recv = lax.all_to_all(pieces, "dp", split_axis=1, concat_axis=0, tiled=False)
    packed, squares = reduce_pack(index, recv)
    gathered = lax.all_to_all(packed, "dp", split_axis=0, concat_axis=0, tiled=True)
    square_sum = lax.psum(squares[0, 0], ("dp", "mp"))
    entries = N * N * BLK * 4
    clip = (1.0 / jnp.sqrt(square_sum / entries + tiny_offset)).reshape(1)
    other = lax.ppermute(gathered[:, 1:2], "mp", CORE_PAIRS)

    own = run_task(occupied[0:1], clip, gathered, factor_state, 0)
    helped = run_task(other_occupied, clip, other, other_pair, 1)
    returned = lax.ppermute(helped, "mp", CORE_PAIRS)
    outgoing = jnp.concatenate([own, returned], axis=1)
    incoming = lax.all_to_all(outgoing, "dp", split_axis=0, concat_axis=0, tiled=True)
    piece = pick(owners, slot_of, incoming)

    column = jnp.stack(spread(piece, 0, 0, 1))
    first = jnp.stack(spread(column[:, :HALF], 0, 1, 0))
    second = jnp.stack(spread(column[:, HALF:], 1, 0, 0))
    first = spread(first, 1, 0, 0)
    second = spread(second, 0, 1, 0)
    place = jnp.stack([myself % 4, (myself // 4) % 4, myself // 16]).astype(jnp.int32)
    directions = place_all(place, first, second)
    next_state = new_state(occupied, clip, gathered, factor_state)
    return directions, next_state


def solution(mesh):
    in_specs = (P("dp", "mp", None, None), P("mp", "dp", None, None, None, None), P("mp", None))
    out_specs = (P("mp", None, None), P("mp", "dp", None, None, None, None))
    return jax.shard_map(shards, mesh=mesh, in_specs=in_specs, out_specs=out_specs, check_vma=False)
```

```python
import functools

import jax
import jax.numpy as jnp
from jax import lax
from jax.experimental import pallas as pl
from jax.experimental.pallas import tpu as pltpu
from jax.sharding import PartitionSpec as P

SLOTS = 2
N = 512
BLK = 10
NDP = 32
PIECE = N // NDP
ROWS = 2 * PIECE
HALF = BLK // 2
TR = 256
SMALL = 16 << 20
F32 = jnp.float32
BF = jnp.bfloat16

decay_rate = 0.95
ridge_term = 0.001
tiny_offset = 1e-06


def dp_pairs(dx, dy, dz):
    pairs = []
    for z in range(2):
        for y in range(4):
            for x in range(4):
                to = ((z + dz) % 2) * 16 + ((y + dy) % 4) * 4 + (x + dx) % 4
                pairs.append((z * 16 + y * 4 + x, to))
    return pairs


CORE_PAIRS = [(0, 1), (1, 0), (2, 3), (3, 2)]


def split(v):
    hi = v.astype(BF)
    return hi, (v - hi.astype(F32)).astype(BF)


def dot(a, b):
    return jnp.dot(a, b, preferred_element_type=F32)


def on_diagonal(r):
    i = lax.broadcasted_iota(jnp.int32, (TR, N), 0) + r * TR
    j = lax.broadcasted_iota(jnp.int32, (TR, N), 1)
    return i == j


def store(ref, rows, v):
    hi, lo = split(v)
    ref[0, rows, :] = hi
    ref[1, rows, :] = lo


def product(a, b, finish):
    for r in range(N // TR):
        rows = pl.ds(r * TR, TR)
        ah = a[0, rows, :]
        al = a[1, rows, :]
        finish(r, rows, dot(ah, b[0]) + (dot(ah, b[1]) + dot(al, b[0])))


def power_eighth(total):
    wide = jnp.full((8, 128), total, F32)
    return (1.0 / jnp.sqrt(jnp.sqrt(jnp.sqrt(wide))))[0:1, 0:1]


def add_kernel(across, place, own, r1, r2, r3, o0, o1, o2, o3, total):
    value = own[...].reshape(4, ROWS, N).astype(F32)
    for other in (r1, r2, r3):
        value += other[...].reshape(4, ROWS, N).astype(F32)
    total[...] = value
    here = place[across]
    for step, out in enumerate((o0, o1, o2, o3)):
        out[0] = total[lax.rem(here + step, 4)]


def add_pieces(place, grads, received, group):
    if group == 0:
        own = pl.BlockSpec((1, 1, 4, ROWS, N), lambda b, p: (b, p[0], 0, 0, 0))
        across = 1
    else:
        own = pl.BlockSpec((1, 4, 1, ROWS, N), lambda b, p: (HALF + b, 0, p[1], 0, 0))
        across = 0
    return pl.pallas_call(
        functools.partial(add_kernel, across),
        grid_spec=pltpu.PrefetchScalarGridSpec(
            num_scalar_prefetch=1,
            grid=(HALF,),
            in_specs=[own] + [pl.BlockSpec((1, 4, ROWS, N), lambda b, p: (b, 0, 0, 0))] * 3,
            out_specs=[pl.BlockSpec((1, ROWS, N), lambda b, p: (b, 0, 0))] * 4,
            scratch_shapes=[pltpu.VMEM((4, ROWS, N), F32)],
        ),
        out_shape=[jax.ShapeDtypeStruct((HALF, ROWS, N), F32)] * 4,
        compiler_params=pltpu.CompilerParams(dimension_semantics=("arbitrary",), vmem_limit_bytes=SMALL),
        cost_estimate=pl.CostEstimate(flops=2_000_000, bytes_accessed=4_000_000, transcendentals=0),
    )(place, grads, *received)


def add_again_kernel(place, *refs):
    keep, send, total = refs[8], refs[9], refs[10]
    for group in range(2):
        a, b, c, d = (ref[0] for ref in refs[4 * group : 4 * group + 4])
        total[group] = (a + b) + (c + d)
    z = place[2]
    near = pl.multiple_of(z * PIECE, PIECE)
    far = pl.multiple_of((1 - z) * PIECE, PIECE)
    keep[:, 0] = total[:, pl.ds(near, PIECE), :]
    send[:, 0] = total[:, pl.ds(far, PIECE), :]


def add_again(place, first, second):
    spec = pl.BlockSpec((2, 1, PIECE, N), lambda b, p: (0, b, 0, 0))
    return pl.pallas_call(
        add_again_kernel,
        grid_spec=pltpu.PrefetchScalarGridSpec(
            num_scalar_prefetch=1,
            grid=(HALF,),
            in_specs=[pl.BlockSpec((1, ROWS, N), lambda b, p: (b, 0, 0))] * 8,
            out_specs=[spec] * 2,
            scratch_shapes=[pltpu.VMEM((2, ROWS, N), F32)],
        ),
        out_shape=[jax.ShapeDtypeStruct((2, HALF, PIECE, N), F32)] * 2,
        compiler_params=pltpu.CompilerParams(dimension_semantics=("arbitrary",), vmem_limit_bytes=SMALL),
        cost_estimate=pl.CostEstimate(flops=1_000_000, bytes_accessed=3_300_000, transcendentals=0),
        name="add_again",
    )(place, *first, *second)


def pack_kernel(index_ref, keep, recv, out_ref, square_ref, total):
    squares = jnp.zeros((PIECE, N), F32)
    for b in range(BLK):
        value = keep[b // HALF, b % HALF] + recv[b // HALF, b % HALF]
        total[b] = value
        squares += value * value
    square_ref[...] = jnp.broadcast_to(jnp.sum(squares), square_ref.shape)

    @pl.loop(0, NDP)
    def _(o):
        for s in range(SLOTS):
            out_ref[o, s] = total[index_ref[s, o]]


def pack(index, keep, recv):
    return pl.pallas_call(
        pack_kernel,
        in_specs=[pl.BlockSpec(memory_space=pltpu.SMEM)] + [pl.BlockSpec(memory_space=pltpu.VMEM)] * 2,
        out_specs=[pl.BlockSpec(memory_space=pltpu.VMEM)] * 2,
        out_shape=[
            jax.ShapeDtypeStruct((NDP, SLOTS, PIECE, N), F32),
            jax.ShapeDtypeStruct((8, 128), F32),
        ],
        scratch_shapes=[pltpu.VMEM((BLK, PIECE, N), F32)],
        compiler_params=pltpu.CompilerParams(vmem_limit_bytes=SMALL),
        cost_estimate=pl.CostEstimate(flops=300_000, bytes_accessed=3_000_000, transcendentals=0),
        name="pack",
    )(index, keep, recv)


def piece_row(device):
    return (device % 4) * 128 + (device // 4 % 4) * ROWS + (device // 16) * PIECE


def task_kernel(occ, clip, own_g, own_old, other_g, other_old, own_dir, other_dir, g2, gt2, full, m, f, p, q, m1, f1, x, u, norms):
    task = pl.program_id(0)

    def halves_to(ref):
        return lambda r, rows, acc: store(ref, rows, acc)

    def factor(r, moving):
        return jnp.where(on_diagonal(r), 1.25, 0.0) - 0.25 * moving

    @pl.when(occ[task] > 0)
    def _():
        @pl.when(task == 0)
        def _():
            for source in range(NDP):
                full[pl.ds(piece_row(source), PIECE), :] = other_g[source, 0] * clip[0]

        @pl.when(task == 1)
        def _():
            for source in range(NDP):
                full[pl.ds(piece_row(source), PIECE), :] = own_g[source, 0] * clip[0]

        g = full[...]
        squares = jnp.sum(g * g)
        store(g2, pl.ds(0, N), g)
        store(gt2, pl.ds(0, N), g.T)

        def root(side, carry):
            def gram(a, b):
                def finish(r, rows, acc):
                    full[rows, :] = (1.0 - decay_rate) * acc + jnp.where(on_diagonal(r), ridge_term, 0.0)

                product(a, b, finish)

            @pl.when(side == 0)
            def _():
                gram(g2, gt2)

            @pl.when(side == 1)
            def _():
                gram(gt2, g2)

            @pl.when(task == 0)
            def _():
                full[...] += decay_rate * other_old[0, 0, 0, side]

            @pl.when(task == 1)
            def _():
                full[...] += decay_rate * own_old[0, 0, 0, side]

            whole = full[...]
            norm2 = jnp.sum(whole * whole)
            norms[side] = norm2
            inverse = (1.0 / jnp.sqrt(jnp.full((8, 128), norm2, F32)))[0:1, 0:1]
            for r in range(N // TR):
                rows = pl.ds(r * TR, TR)
                moving = full[rows, :] * inverse
                store(m, rows, moving)
                store(f, rows, factor(r, moving))

            def first(r, rows, acc):
                store(m1, rows, acc)
                store(f1, rows, factor(r, acc))

            product(f, f, halves_to(p))
            product(p, p, halves_to(q))
            product(q, m, first)
            product(f, f1, halves_to(x))
            product(f1, f1, halves_to(p))
            product(p, p, halves_to(q))
            product(q, m1, lambda r, rows, acc: store(m, rows, factor(r, acc)))
            product(x, m, halves_to(u.at[side]))
            return carry

        lax.fori_loop(0, 2, root, 0)

        def last(r, rows, acc):
            full[rows, :] = acc

        product(u.at[0], g2, halves_to(p))
        product(p, u.at[1], last)
        precond = full[...] * (power_eighth(norms[0]) * power_eighth(norms[1]))
        entries = N * N
        actual = jnp.full((8, 128), jnp.sum(precond * precond) / entries + tiny_offset, F32)
        target = jnp.full((8, 128), squares / entries + tiny_offset, F32)
        graft = (jnp.sqrt(target) / jnp.sqrt(actual))[0:1, 0:1]
        full[...] = precond * graft

        @pl.when(task == 0)
        def _():
            for device in range(NDP):
                other_dir[device, 0] = full[pl.ds(piece_row(device), PIECE), :].astype(BF)

        @pl.when(task == 1)
        def _():
            for device in range(NDP):
                own_dir[device, 0] = full[pl.ds(piece_row(device), PIECE), :].astype(BF)


def pair():
    return pltpu.VMEM((2, N, N), BF)


def run_tasks(occupied, clip, own_g, own_pairs, other_g, other_pair):
    result = jax.ShapeDtypeStruct((NDP, 1, PIECE, N), BF)
    return pl.pallas_call(
        task_kernel,
        grid=(2,),
        in_specs=[pl.BlockSpec(memory_space=pltpu.SMEM)] * 2 + [pl.BlockSpec(memory_space=pltpu.VMEM)] * 4,
        out_specs=[pl.BlockSpec(memory_space=pltpu.VMEM)] * 2,
        out_shape=[result, result],
        scratch_shapes=[pair(), pair(), pltpu.VMEM((N, N), F32)]
        + [pair() for _ in range(7)]
        + [pltpu.VMEM((2, 2, N, N), BF), pltpu.SMEM((2,), F32)],
        compiler_params=pltpu.CompilerParams(dimension_semantics=("arbitrary",), vmem_limit_bytes=36 << 20),
        cost_estimate=pl.CostEstimate(flops=16_000_000_000, bytes_accessed=3_500_000, transcendentals=0),
        name="tasks",
    )(occupied, clip, own_g, own_pairs, other_g, other_pair)


def state_kernel(occ, clip, g_ref, old_ref, new_ref, full, g2, gt2):
    s = pl.program_id(0)

    @pl.when(occ[s] > 0)
    def _():
        for source in range(NDP):
            full[pl.ds(piece_row(source), PIECE), :] = g_ref[source, 0] * clip[0]
        g = full[...]
        store(g2, pl.ds(0, N), g)
        store(gt2, pl.ds(0, N), g.T)

        def mix(side):
            def finish(r, rows, acc):
                new_ref[0, 0, 0, side, rows, :] = (
                    decay_rate * old_ref[0, 0, 0, side, rows, :] + (1.0 - decay_rate) * acc
                )

            return finish

        product(g2, gt2, mix(0))
        product(gt2, g2, mix(1))

    @pl.when(occ[s] <= 0)
    def _():
        new_ref[...] = old_ref[...]


def new_state(occupied, clip, gathered, pairs):
    block = pl.BlockSpec((1, 1, 1, 2, N, N), lambda s: (0, 0, s, 0, 0, 0))
    return pl.pallas_call(
        state_kernel,
        grid=(SLOTS,),
        in_specs=[
            pl.BlockSpec(memory_space=pltpu.SMEM),
            pl.BlockSpec(memory_space=pltpu.SMEM),
            pl.BlockSpec((NDP, 1, PIECE, N), lambda s: (0, s, 0, 0)),
            block,
        ],
        out_specs=block,
        out_shape=jax.ShapeDtypeStruct(pairs.shape, F32),
        scratch_shapes=[pltpu.VMEM((N, N), F32), pair(), pair()],
        compiler_params=pltpu.CompilerParams(dimension_semantics=("arbitrary",), vmem_limit_bytes=SMALL),
        cost_estimate=pl.CostEstimate(flops=3_000_000_000, bytes_accessed=10_000_000, transcendentals=0),
        name="state",
    )(occupied, clip, gathered, pairs)


def pick_kernel(owner, slot, recv_ref, out_ref):
    for b in range(BLK):
        out_ref[b] = recv_ref[owner[b], slot[b]]


def pick(owner, slot, recv):
    return pl.pallas_call(
        pick_kernel,
        in_specs=[pl.BlockSpec(memory_space=pltpu.SMEM)] * 2 + [pl.BlockSpec(memory_space=pltpu.VMEM)],
        out_specs=pl.BlockSpec(memory_space=pltpu.VMEM),
        out_shape=jax.ShapeDtypeStruct((BLK, PIECE, N), BF),
        compiler_params=pltpu.CompilerParams(vmem_limit_bytes=SMALL),
        name="pick",
    )(owner, slot, recv)


def place_kernel(place, *refs):
    first, second, out, sems = refs[:4], refs[4:8], refs[8], refs[9]
    x, y, z = place[0], place[1], place[2]
    copies = []
    for far in range(4):
        for near in range(4):
            for dz in range(2):
                for group, dx, dy, ref in ((0, far, near, first[far]), (1, near, far, second[far])):
                    row = lax.rem(z + dz, 2) * PIECE + lax.rem(y + 4 - dy, 4) * ROWS + lax.rem(x + 4 - dx, 4) * 128
                    row = pl.multiple_of(row, PIECE)
                    copies.append(
                        pltpu.make_async_copy(
                            ref.at[near, dz],
                            out.at[pl.ds(group * HALF, HALF), pl.ds(row, PIECE), :],
                            sems.at[len(copies)],
                        )
                    )
    for copy in copies:
        copy.start()
    for copy in copies:
        copy.wait()


def place_all(place, first, second):
    return pl.pallas_call(
        place_kernel,
        in_specs=[pl.BlockSpec(memory_space=pltpu.SMEM)] + [pl.BlockSpec(memory_space=pltpu.VMEM)] * 8,
        out_specs=pl.BlockSpec(memory_space=pl.ANY),
        out_shape=jax.ShapeDtypeStruct((BLK, N, N), BF),
        scratch_shapes=[pltpu.SemaphoreType.DMA((64,))],
        compiler_params=pltpu.CompilerParams(vmem_limit_bytes=SMALL),
        name="place",
    )(place, *first, *second)


def spread(v, dx, dy, dz):
    steps = 2 if dz else 4
    return [v] + [lax.ppermute(v, "dp", dp_pairs(dx * k, dy * k, dz * k)) for k in range(1, steps)]


def owner_slots(owners):
    positions = jnp.arange(owners.shape[0], dtype=jnp.int32)
    same_owner = owners[:, None] == owners[None, :]
    earlier = positions[None, :] < positions[:, None]
    return jnp.sum((same_owner & earlier).astype(jnp.int32), axis=1)


def shards(gradients, factor_state, block_owner):
    owners = block_owner[0]
    myself = lax.axis_index("dp")
    slot_of = owner_slots(owners)
    positions = jnp.arange(BLK, dtype=jnp.int32)
    slots = jnp.arange(SLOTS, dtype=jnp.int32)
    devices = jnp.arange(NDP, dtype=jnp.int32)
    match = (owners == devices[None, :, None]) & (slot_of == slots[:, None, None])
    index = jnp.sum(jnp.where(match, positions, 0), axis=2)
    mine = (owners == myself) & (slot_of == slots[:, None])
    occupied = jnp.max(mine.astype(jnp.int32), axis=1)
    other_occupied = lax.ppermute(occupied[1:2], "mp", CORE_PAIRS)
    other_pair = lax.ppermute(factor_state[:, :, 1:2], "mp", CORE_PAIRS)

    place = jnp.stack([myself % 4, (myself // 4) % 4, myself // 16]).astype(jnp.int32)
    grads = gradients[0].reshape(BLK, 4, 4, ROWS, N)
    first, second = [], []
    zero = jnp.int32(0)
    for k in range(1, 4):
        piece = lax.dynamic_slice(grads, (zero, (place[0] + k) % 4, zero, zero, zero), (HALF, 1, 4, ROWS, N))
        first.append(lax.ppermute(piece.reshape(HALF, 4, ROWS, N), "dp", dp_pairs(k, 0, 0)))
        start = (jnp.int32(HALF), zero, (place[1] + k) % 4, zero, zero)
        piece = lax.dynamic_slice(grads, start, (HALF, 4, 1, ROWS, N))
        second.append(lax.ppermute(piece.reshape(HALF, 4, ROWS, N), "dp", dp_pairs(0, k, 0)))
    first = add_pieces(place, grads, first, 0)
    second = add_pieces(place, grads, second, 1)
    first = [first[0]] + [lax.ppermute(first[k], "dp", dp_pairs(0, k, 0)) for k in range(1, 4)]
    second = [second[0]] + [lax.ppermute(second[k], "dp", dp_pairs(k, 0, 0)) for k in range(1, 4)]
    keep, send = add_again(place, first, second)
    packed, squares = pack(index, keep, lax.ppermute(send, "dp", dp_pairs(0, 0, 1)))
    gathered = lax.all_to_all(packed, "dp", split_axis=0, concat_axis=0, tiled=True)
    hops = [("mp", bit, 4) for bit in (1, 2)] + [("dp", bit, NDP) for bit in (1, 2, 4, 8, 16)]
    for axis, bit, size in hops:
        squares = squares + lax.ppermute(squares, axis, [(i, i ^ bit) for i in range(size)])
    square_sum = squares[0, 0]
    entries = N * N * BLK * 4
    clip = (1.0 / jnp.sqrt(square_sum / entries + tiny_offset)).reshape(1)
    other = lax.ppermute(gathered[:, 1:2], "mp", CORE_PAIRS)

    tasks = jnp.concatenate([other_occupied, occupied[0:1]])
    own, helped = run_tasks(tasks, clip, gathered, factor_state, other, other_pair)
    returned = lax.ppermute(helped, "mp", CORE_PAIRS)
    outgoing = jnp.concatenate([own, returned], axis=1)
    incoming = lax.all_to_all(outgoing, "dp", split_axis=0, concat_axis=0, tiled=True)
    piece = pick(owners, slot_of, incoming)

    column = jnp.stack(spread(piece, 0, 0, 1))
    first = jnp.stack(spread(column[:, :HALF], 0, 1, 0))
    second = jnp.stack(spread(column[:, HALF:], 1, 0, 0))
    first = spread(first, 1, 0, 0)
    second = spread(second, 0, 1, 0)
    directions = place_all(place, first, second)
    next_state = new_state(occupied, clip, gathered, factor_state)
    return directions, next_state


def solution(mesh):
    in_specs = (P("dp", "mp", None, None), P("mp", "dp", None, None, None, None), P("mp", None))
    out_specs = (P("mp", None, None), P("mp", "dp", None, None, None, None))
    return jax.shard_map(shards, mesh=mesh, in_specs=in_specs, out_specs=out_specs, check_vma=False)
```

```python
import functools

import jax
import jax.numpy as jnp
from jax import lax
from jax.experimental import pallas as pl
from jax.experimental.pallas import tpu as pltpu
from jax.sharding import PartitionSpec as P

SLOTS = 2
N = 512
BLK = 10
NDP = 32
PIECE = N // NDP
ROWS = 2 * PIECE
CHUNK = PIECE * N // 128
MESSAGE = SLOTS * CHUNK + 8
ENTRIES = N * N * BLK * 4
HALF = BLK // 2
TR = 256
SMALL = 16 << 20
F32 = jnp.float32
BF = jnp.bfloat16

decay_rate = 0.95
ridge_term = 0.001
tiny_offset = 1e-06


def dp_pairs(dx, dy, dz):
    pairs = []
    for z in range(2):
        for y in range(4):
            for x in range(4):
                to = ((z + dz) % 2) * 16 + ((y + dy) % 4) * 4 + (x + dx) % 4
                pairs.append((z * 16 + y * 4 + x, to))
    return pairs


CORE_PAIRS = [(0, 1), (1, 0), (2, 3), (3, 2)]


def split(v):
    hi = v.astype(BF)
    return hi, (v - hi.astype(F32)).astype(BF)


def dot(a, b):
    return jnp.dot(a, b, preferred_element_type=F32)


def on_diagonal(r):
    i = lax.broadcasted_iota(jnp.int32, (TR, N), 0) + r * TR
    j = lax.broadcasted_iota(jnp.int32, (TR, N), 1)
    return i == j


def store(ref, rows, v):
    hi, lo = split(v)
    ref[0, rows, :] = hi
    ref[1, rows, :] = lo


def product(a, b, finish):
    for r in range(N // TR):
        rows = pl.ds(r * TR, TR)
        ah = a[0, rows, :]
        al = a[1, rows, :]
        finish(r, rows, dot(ah, b[0]) + (dot(ah, b[1]) + dot(al, b[0])))


def power_eighth(total):
    wide = jnp.full((8, 128), total, F32)
    return (1.0 / jnp.sqrt(jnp.sqrt(jnp.sqrt(wide))))[0:1, 0:1]


def add_kernel(across, place, own, r1, r2, r3, *outs):
    here = place[across]

    @pl.loop(0, HALF)
    def _(b):
        for step, out in enumerate(outs):
            j = lax.rem(here + step, 4)
            out[b] = (own[b, j].astype(F32) + r1[b, j].astype(F32)) + (r2[b, j].astype(F32) + r3[b, j].astype(F32))


def add_pieces(place, pieces, across):
    return pl.pallas_call(
        functools.partial(add_kernel, across),
        in_specs=[pl.BlockSpec(memory_space=pltpu.SMEM)] + [pl.BlockSpec(memory_space=pltpu.VMEM)] * 4,
        out_specs=[pl.BlockSpec(memory_space=pltpu.VMEM)] * 4,
        out_shape=[jax.ShapeDtypeStruct((HALF, ROWS, N), F32)] * 4,
        compiler_params=pltpu.CompilerParams(vmem_limit_bytes=SMALL),
        cost_estimate=pl.CostEstimate(flops=2_000_000, bytes_accessed=4_000_000, transcendentals=0),
    )(place, *pieces)


def add_again_kernel(place, *refs):
    keep, send, total = refs[8], refs[9], refs[10]
    for group in range(2):
        a, b, c, d = (ref[0] for ref in refs[4 * group : 4 * group + 4])
        total[group] = (a + b) + (c + d)
    z = place[2]
    near = pl.multiple_of(z * PIECE, PIECE)
    far = pl.multiple_of((1 - z) * PIECE, PIECE)
    keep[:, 0] = total[:, pl.ds(near, PIECE), :]
    send[:, 0] = total[:, pl.ds(far, PIECE), :]


def add_again(place, first, second):
    spec = pl.BlockSpec((2, 1, PIECE, N), lambda b, p: (0, b, 0, 0))
    return pl.pallas_call(
        add_again_kernel,
        grid_spec=pltpu.PrefetchScalarGridSpec(
            num_scalar_prefetch=1,
            grid=(HALF,),
            in_specs=[pl.BlockSpec((1, ROWS, N), lambda b, p: (b, 0, 0))] * 8,
            out_specs=[spec] * 2,
            scratch_shapes=[pltpu.VMEM((2, ROWS, N), F32)],
        ),
        out_shape=[jax.ShapeDtypeStruct((2, HALF, PIECE, N), F32)] * 2,
        compiler_params=pltpu.CompilerParams(dimension_semantics=("arbitrary",), vmem_limit_bytes=SMALL),
        cost_estimate=pl.CostEstimate(flops=1_000_000, bytes_accessed=3_300_000, transcendentals=0),
        name="add_again",
    )(place, *first, *second)


def pack_kernel(index_ref, keep, recv, out_ref, total):
    squares = jnp.zeros((PIECE, N), F32)
    for b in range(BLK):
        value = keep[b // HALF, b % HALF] + recv[b // HALF, b % HALF]
        for c in range(4):
            total[b, pl.ds(c * PIECE, PIECE), :] = value[:, c * 128 : (c + 1) * 128]
        squares += value * value
    square = jnp.broadcast_to(jnp.sum(squares), (8, 128))

    @pl.loop(0, NDP)
    def _(o):
        for s in range(SLOTS):
            out_ref[o, pl.ds(s * CHUNK, CHUNK), :] = total[index_ref[s, o]]
        out_ref[o, pl.ds(SLOTS * CHUNK, 8), :] = square


def pack(index, keep, recv):
    return pl.pallas_call(
        pack_kernel,
        in_specs=[pl.BlockSpec(memory_space=pltpu.SMEM)] + [pl.BlockSpec(memory_space=pltpu.VMEM)] * 2,
        out_specs=pl.BlockSpec(memory_space=pltpu.VMEM),
        out_shape=jax.ShapeDtypeStruct((NDP, MESSAGE, 128), F32),
        scratch_shapes=[pltpu.VMEM((BLK, CHUNK, 128), F32)],
        compiler_params=pltpu.CompilerParams(vmem_limit_bytes=SMALL),
        cost_estimate=pl.CostEstimate(flops=300_000, bytes_accessed=3_000_000, transcendentals=0),
        name="pack",
    )(index, keep, recv)


def unpack(full, ref, offset, scale):
    for source in range(NDP):
        for c in range(4):
            piece = ref[source, pl.ds(offset + c * PIECE, PIECE), :]
            full[pl.ds(piece_row(source), PIECE), pl.ds(c * 128, 128)] = piece * scale


def clip_of(sums):
    total = (sums[0][...] + sums[1][...]) + (sums[2][...] + sums[3][...])
    return (1.0 / jnp.sqrt(total / ENTRIES + tiny_offset))[0:1, 0:1]


def piece_row(device):
    return (device % 4) * 128 + (device // 4 % 4) * ROWS + (device // 16) * PIECE


def task_kernel(occ, s0, s1, s2, s3, own_g, own_old, other_g, other_old, own_dir, other_dir, g2, gt2, full, m, f, p, q, m1, f1, x, u, old, norms, sem):
    task = pl.program_id(0)

    def halves_to(ref):
        return lambda r, rows, acc: store(ref, rows, acc)

    def factor(r, moving):
        return jnp.where(on_diagonal(r), 1.25, 0.0) - 0.25 * moving

    @pl.when(occ[task] > 0)
    def _():
        clip = clip_of((s0, s1, s2, s3))

        @pl.when(task == 0)
        def _():
            pltpu.make_async_copy(other_old.at[0, 0, 0], old, sem).start()
            unpack(full, other_g, 0, clip)

        @pl.when(task == 1)
        def _():
            pltpu.make_async_copy(own_old.at[0, 0, 0], old, sem).start()
            unpack(full, own_g, 0, clip)

        g = full[...]
        squares = jnp.sum(g * g)
        store(g2, pl.ds(0, N), g)
        store(gt2, pl.ds(0, N), g.T)

        def root(side, carry):
            def gram(a, b):
                def finish(r, rows, acc):
                    full[rows, :] = (1.0 - decay_rate) * acc + jnp.where(on_diagonal(r), ridge_term, 0.0)

                product(a, b, finish)

            @pl.when(side == 0)
            def _():
                gram(g2, gt2)
                pltpu.make_async_copy(own_old.at[0, 0, 0], old, sem).wait()

            @pl.when(side == 1)
            def _():
                gram(gt2, g2)

            full[...] += decay_rate * old[side]
            whole = full[...]
            norm2 = jnp.sum(whole * whole)
            norms[side] = norm2
            inverse = (1.0 / jnp.sqrt(jnp.full((8, 128), norm2, F32)))[0:1, 0:1]
            for r in range(N // TR):
                rows = pl.ds(r * TR, TR)
                moving = full[rows, :] * inverse
                store(m, rows, moving)
                store(f, rows, factor(r, moving))

            def first(r, rows, acc):
                store(m1, rows, acc)
                store(f1, rows, factor(r, acc))

            product(f, f, halves_to(p))
            product(p, p, halves_to(q))
            product(q, m, first)
            product(f, f1, halves_to(x))
            product(f1, f1, halves_to(p))
            product(p, p, halves_to(q))
            product(q, m1, lambda r, rows, acc: store(m, rows, factor(r, acc)))
            product(x, m, halves_to(u.at[side]))
            return carry

        lax.fori_loop(0, 2, root, 0)

        def last(r, rows, acc):
            full[rows, :] = acc

        product(u.at[0], g2, halves_to(p))
        product(p, u.at[1], last)
        precond = full[...] * (power_eighth(norms[0]) * power_eighth(norms[1]))
        entries = N * N
        actual = jnp.full((8, 128), jnp.sum(precond * precond) / entries + tiny_offset, F32)
        target = jnp.full((8, 128), squares / entries + tiny_offset, F32)
        graft = (jnp.sqrt(target) / jnp.sqrt(actual))[0:1, 0:1]
        full[...] = precond * graft

        @pl.when(task == 0)
        def _():
            for device in range(NDP):
                other_dir[device, 0] = full[pl.ds(piece_row(device), PIECE), :].astype(BF)

        @pl.when(task == 1)
        def _():
            for device in range(NDP):
                own_dir[device, 0] = full[pl.ds(piece_row(device), PIECE), :].astype(BF)


def pair():
    return pltpu.VMEM((2, N, N), BF)


def run_tasks(occupied, sums, own_g, own_pairs, other_g, other_pair):
    result = jax.ShapeDtypeStruct((NDP, 1, PIECE, N), BF)
    return pl.pallas_call(
        task_kernel,
        grid=(2,),
        in_specs=[pl.BlockSpec(memory_space=pltpu.SMEM)]
        + [pl.BlockSpec(memory_space=pltpu.VMEM)] * 4
        + [pl.BlockSpec(memory_space=space) for space in (pltpu.VMEM, pltpu.HBM, pltpu.VMEM, pltpu.HBM)],
        out_specs=[pl.BlockSpec(memory_space=pltpu.VMEM)] * 2,
        out_shape=[result, result],
        scratch_shapes=[pair(), pair(), pltpu.VMEM((N, N), F32)]
        + [pair() for _ in range(7)]
        + [pltpu.VMEM((2, 2, N, N), BF), pltpu.VMEM((2, N, N), F32), pltpu.SMEM((2,), F32), pltpu.SemaphoreType.DMA],
        compiler_params=pltpu.CompilerParams(dimension_semantics=("arbitrary",), vmem_limit_bytes=36 << 20),
        cost_estimate=pl.CostEstimate(flops=16_000_000_000, bytes_accessed=3_500_000, transcendentals=0),
        name="tasks",
    )(occupied, *sums, own_g, own_pairs, other_g, other_pair)


def state_kernel(occ, s0, s1, s2, s3, g_ref, old_ref, new_ref, full, g2, gt2):
    s = pl.program_id(0)

    @pl.when(occ[s] > 0)
    def _():
        unpack(full, g_ref, pl.multiple_of(s * CHUNK, CHUNK), clip_of((s0, s1, s2, s3)))
        g = full[...]
        store(g2, pl.ds(0, N), g)
        store(gt2, pl.ds(0, N), g.T)

        def mix(side):
            def finish(r, rows, acc):
                new_ref[0, 0, 0, side, rows, :] = (
                    decay_rate * old_ref[0, 0, 0, side, rows, :] + (1.0 - decay_rate) * acc
                )

            return finish

        product(g2, gt2, mix(0))
        product(gt2, g2, mix(1))

    @pl.when(occ[s] <= 0)
    def _():
        new_ref[...] = old_ref[...]


def new_state(occupied, sums, gathered, pairs):
    block = pl.BlockSpec((1, 1, 1, 2, N, N), lambda s: (0, 0, s, 0, 0, 0))
    return pl.pallas_call(
        state_kernel,
        grid=(SLOTS,),
        in_specs=[
            pl.BlockSpec(memory_space=pltpu.SMEM),
        ]
        + [pl.BlockSpec(memory_space=pltpu.VMEM)] * 5
        + [block],
        out_specs=block,
        out_shape=jax.ShapeDtypeStruct(pairs.shape, F32),
        scratch_shapes=[pltpu.VMEM((N, N), F32), pair(), pair()],
        compiler_params=pltpu.CompilerParams(dimension_semantics=("arbitrary",), vmem_limit_bytes=SMALL),
        cost_estimate=pl.CostEstimate(flops=3_000_000_000, bytes_accessed=10_000_000, transcendentals=0),
        name="state",
    )(occupied, *sums, gathered, pairs)


def pick_kernel(owner, slot, recv_ref, out_ref):
    for b in range(BLK):
        out_ref[b] = recv_ref[owner[b], slot[b]]


def pick(owner, slot, recv):
    return pl.pallas_call(
        pick_kernel,
        in_specs=[pl.BlockSpec(memory_space=pltpu.SMEM)] * 2 + [pl.BlockSpec(memory_space=pltpu.VMEM)],
        out_specs=pl.BlockSpec(memory_space=pltpu.VMEM),
        out_shape=jax.ShapeDtypeStruct((BLK, PIECE, N), BF),
        compiler_params=pltpu.CompilerParams(vmem_limit_bytes=SMALL),
        name="pick",
    )(owner, slot, recv)


def place_kernel(place, *refs):
    groups, out, sems = (refs[:5], refs[5:10]), refs[10], refs[11]
    x, y, z = place[0], place[1], place[2]
    copies = []
    for far in range(4):
        for near in range(4):
            for dz in range(2):
                for group, dx, dy in ((0, far, near), (1, near, far)):
                    here, back, low, high, front = groups[group]
                    source = (here, back, low if near < 2 else high, front)[far]
                    row = lax.rem(z + dz, 2) * PIECE + lax.rem(y + 4 - dy, 4) * ROWS + lax.rem(x + 4 - dx, 4) * 128
                    copies.append(
                        pltpu.make_async_copy(
                            source.at[near % 2 if far == 2 else near, dz],
                            out.at[pl.ds(group * HALF, HALF), pl.ds(pl.multiple_of(row, PIECE), PIECE), :],
                            sems.at[len(copies)],
                        )
                    )
    for copy in copies:
        copy.start()
    for copy in copies:
        copy.wait()


def place_all(place, first, second):
    return pl.pallas_call(
        place_kernel,
        in_specs=[pl.BlockSpec(memory_space=pltpu.SMEM)] + [pl.BlockSpec(memory_space=pltpu.VMEM)] * 10,
        out_specs=pl.BlockSpec(memory_space=pl.ANY),
        out_shape=jax.ShapeDtypeStruct((BLK, N, N), BF),
        scratch_shapes=[pltpu.SemaphoreType.DMA((64,))],
        compiler_params=pltpu.CompilerParams(vmem_limit_bytes=SMALL),
        name="place",
    )(place, *first, *second)


def around(v, dx, dy):
    ahead, behind = dp_pairs(dx, dy, 0), dp_pairs(3 * dx, 3 * dy, 0)
    back = lax.ppermute(v, "dp", ahead)
    front = lax.ppermute(v, "dp", behind)
    return [v, back, lax.ppermute(back[:2], "dp", ahead), lax.ppermute(front[2:], "dp", behind), front]


def spread(v, dx, dy, dz):
    steps = 2 if dz else 4
    return [v] + [lax.ppermute(v, "dp", dp_pairs(dx * k, dy * k, dz * k)) for k in range(1, steps)]


def owner_slots(owners):
    positions = jnp.arange(owners.shape[0], dtype=jnp.int32)
    same_owner = owners[:, None] == owners[None, :]
    earlier = positions[None, :] < positions[:, None]
    return jnp.sum((same_owner & earlier).astype(jnp.int32), axis=1)


def shards(gradients, factor_state, block_owner):
    owners = block_owner[0]
    myself = lax.axis_index("dp")
    slot_of = owner_slots(owners)
    positions = jnp.arange(BLK, dtype=jnp.int32)
    slots = jnp.arange(SLOTS, dtype=jnp.int32)
    devices = jnp.arange(NDP, dtype=jnp.int32)
    match = (owners == devices[None, :, None]) & (slot_of == slots[:, None, None])
    index = jnp.sum(jnp.where(match, positions, 0), axis=2)
    mine = (owners == myself) & (slot_of == slots[:, None])
    occupied = jnp.max(mine.astype(jnp.int32), axis=1)
    other_occupied = lax.ppermute(occupied[1:2], "mp", CORE_PAIRS)
    other_pair = lax.ppermute(factor_state[:, :, 1:2], "mp", CORE_PAIRS)

    place = jnp.stack([myself % 4, (myself // 4) % 4, myself // 16]).astype(jnp.int32)
    grads = gradients[0].reshape(BLK, 4, 4, ROWS, N)
    first, second = [None] * 4, [None] * 4
    zero = jnp.int32(0)
    for k in (1, 2, 3, 0):
        start = (zero, (place[0] + k) % 4, zero, zero, zero)
        piece = lax.dynamic_slice(grads, start, (HALF, 1, 4, ROWS, N)).reshape(HALF, 4, ROWS, N)
        grads, piece = lax.optimization_barrier((grads, piece))
        first[k] = lax.ppermute(piece, "dp", dp_pairs(k, 0, 0)) if k else piece
        start = (jnp.int32(HALF), zero, (place[1] + k) % 4, zero, zero)
        piece = lax.dynamic_slice(grads, start, (HALF, 4, 1, ROWS, N)).reshape(HALF, 4, ROWS, N)
        grads, piece = lax.optimization_barrier((grads, piece))
        second[k] = lax.ppermute(piece, "dp", dp_pairs(0, k, 0)) if k else piece
    first = add_pieces(place, first, 1)
    second = add_pieces(place, second, 0)
    first = [first[0]] + [lax.ppermute(first[k], "dp", dp_pairs(0, k, 0)) for k in range(1, 4)]
    second = [second[0]] + [lax.ppermute(second[k], "dp", dp_pairs(k, 0, 0)) for k in range(1, 4)]
    keep, send = add_again(place, first, second)
    tasks = jnp.concatenate([other_occupied, occupied[0:1]])
    index, tasks, occupied = lax.optimization_barrier((index, tasks, occupied))
    packed = pack(index, keep, lax.ppermute(send, "dp", dp_pairs(0, 0, 1)))
    gathered = lax.all_to_all(packed, "dp", split_axis=0, concat_axis=0, tiled=True)
    other = lax.ppermute(gathered[:, CHUNK : 2 * CHUNK], "mp", CORE_PAIRS)
    squares = jnp.sum(gathered[:, SLOTS * CHUNK :], axis=0)
    sums = [squares] + [lax.ppermute(squares, "mp", [(i, i ^ bit) for i in range(4)]) for bit in (1, 2, 3)]
    own, helped = run_tasks(tasks, sums, gathered, factor_state, other, other_pair)
    returned = lax.ppermute(helped, "mp", CORE_PAIRS)
    outgoing = jnp.concatenate([own, returned], axis=1)
    incoming = lax.all_to_all(outgoing, "dp", split_axis=0, concat_axis=0, tiled=True)
    piece = pick(owners, slot_of, incoming)

    column = jnp.stack(spread(piece, 0, 0, 1))
    first = jnp.stack(spread(column[:, :HALF], 0, 1, 0))
    second = jnp.stack(spread(column[:, HALF:], 1, 0, 0))
    first = around(first, 1, 0)
    second = around(second, 0, 1)
    directions = place_all(place, first, second)
    next_state = new_state(occupied, sums, gathered, factor_state)
    return directions, next_state


def solution(mesh):
    in_specs = (P("dp", "mp", None, None), P("mp", "dp", None, None, None, None), P("mp", None))
    out_specs = (P("mp", None, None), P("mp", "dp", None, None, None, None))
    return jax.shard_map(shards, mesh=mesh, in_specs=in_specs, out_specs=out_specs, check_vma=False)
```

```python
import functools

import jax
import jax.numpy as jnp
from jax import lax
from jax.experimental import pallas as pl
from jax.experimental.pallas import tpu as pltpu
from jax.sharding import PartitionSpec as P

SLOTS = 2
N = 512
BLK = 10
NDP = 32
PIECE = N // NDP
ROWS = 2 * PIECE
CHUNK = PIECE * N // 128
MESSAGE = SLOTS * CHUNK + 8
ENTRIES = N * N * BLK * 4
HALF = BLK // 2
TR = 256
SMALL = 16 << 20
F32 = jnp.float32
BF = jnp.bfloat16

decay_rate = 0.95
ridge_term = 0.001
tiny_offset = 1e-06


def dp_pairs(dx, dy, dz):
    pairs = []
    for z in range(2):
        for y in range(4):
            for x in range(4):
                to = ((z + dz) % 2) * 16 + ((y + dy) % 4) * 4 + (x + dx) % 4
                pairs.append((z * 16 + y * 4 + x, to))
    return pairs


CORE_PAIRS = [(0, 1), (1, 0), (2, 3), (3, 2)]


def split(v):
    hi = v.astype(BF)
    return hi, (v - hi.astype(F32)).astype(BF)


def dot(a, b):
    return jnp.dot(a, b, preferred_element_type=F32)


def scaled_eye(value):
    i = lax.broadcasted_iota(jnp.int32, (TR, TR), 0)
    j = lax.broadcasted_iota(jnp.int32, (TR, TR), 1)
    return jnp.where(i == j, value, 0.0)


def store(ref, rows, v):
    hi, lo = split(v)
    ref[0, rows, :] = hi
    ref[1, rows, :] = lo


def area(i, j):
    return pl.ds(i * TR, TR), pl.ds(j * TR, TR)


def store_block(ref, i, j, v):
    rows, columns = area(i, j)
    hi, lo = split(v)
    ref[0, rows, columns] = hi
    ref[1, rows, columns] = lo


def product(a, b, finish):
    for r in range(N // TR):
        rows = pl.ds(r * TR, TR)
        ah = a[0, rows, :]
        al = a[1, rows, :]
        finish(r, rows, dot(ah, b[0]) + (dot(ah, b[1]) + dot(al, b[0])))


def symmetric(a, b, finish):
    top = pl.ds(0, TR)
    low = pl.ds(TR, TR)
    ah = a[0, top, :]
    al = a[1, top, :]
    acc = dot(ah, b[0]) + (dot(ah, b[1]) + dot(al, b[0]))
    finish(0, 0, acc[:, :TR])
    side = acc[:, TR:]
    finish(0, 1, side)
    finish(1, 0, side.T)
    ah = a[0, low, :]
    al = a[1, low, :]
    finish(1, 1, dot(ah, b[0, :, low]) + (dot(ah, b[1, :, low]) + dot(al, b[0, :, low])))


def power_eighth(total):
    wide = jnp.full((8, 128), total, F32)
    return (1.0 / jnp.sqrt(jnp.sqrt(jnp.sqrt(wide))))[0:1, 0:1]


def cut_kernel(place, grads, *refs):
    outs, sems = refs[:6], refs[6]
    copies = []
    for k in range(1, 4):
        x = lax.rem(place[0] + k, 4)
        y = lax.rem(place[1] + k, 4)
        copies.append(pltpu.make_async_copy(grads.at[pl.ds(0, HALF), x], outs[k - 1], sems.at[k - 1]))
        copies.append(pltpu.make_async_copy(grads.at[pl.ds(HALF, HALF), :, y], outs[k + 2], sems.at[k + 2]))
    for copy in copies:
        copy.start()
    for copy in copies:
        copy.wait()


def cut(place, grads):
    return pl.pallas_call(
        cut_kernel,
        in_specs=[pl.BlockSpec(memory_space=pltpu.SMEM), pl.BlockSpec(memory_space=pltpu.HBM)],
        out_specs=[pl.BlockSpec(memory_space=pltpu.VMEM)] * 6,
        out_shape=[jax.ShapeDtypeStruct((HALF, 4, ROWS, N), BF)] * 6,
        scratch_shapes=[pltpu.SemaphoreType.DMA((6,))],
        compiler_params=pltpu.CompilerParams(vmem_limit_bytes=SMALL),
        name="cut",
    )(place, pltpu.with_memory_space_constraint(grads, pltpu.HBM))


def add_kernel(across, place, own, r1, r2, r3, *outs):
    here = place[across]

    @pl.loop(0, HALF)
    def _(b):
        for step, out in enumerate(outs):
            j = lax.rem(here + step, 4)
            out[b] = (own[b, j].astype(F32) + r1[b, j].astype(F32)) + (r2[b, j].astype(F32) + r3[b, j].astype(F32))


def add_pieces(place, pieces, across):
    return pl.pallas_call(
        functools.partial(add_kernel, across),
        in_specs=[pl.BlockSpec(memory_space=pltpu.SMEM)] + [pl.BlockSpec(memory_space=pltpu.VMEM)] * 4,
        out_specs=[pl.BlockSpec(memory_space=pltpu.VMEM)] * 4,
        out_shape=[jax.ShapeDtypeStruct((HALF, ROWS, N), F32)] * 4,
        compiler_params=pltpu.CompilerParams(vmem_limit_bytes=SMALL),
        cost_estimate=pl.CostEstimate(flops=2_000_000, bytes_accessed=4_000_000, transcendentals=0),
    )(place, *pieces)


def add_again_kernel(place, *refs):
    keep, send, total = refs[8], refs[9], refs[10]
    for group in range(2):
        a, b, c, d = (ref[0] for ref in refs[4 * group : 4 * group + 4])
        total[group] = (a + b) + (c + d)
    z = place[2]
    near = pl.multiple_of(z * PIECE, PIECE)
    far = pl.multiple_of((1 - z) * PIECE, PIECE)
    keep[:, 0] = total[:, pl.ds(near, PIECE), :]
    send[:, 0] = total[:, pl.ds(far, PIECE), :]


def add_again(place, first, second):
    spec = pl.BlockSpec((2, 1, PIECE, N), lambda b, p: (0, b, 0, 0))
    return pl.pallas_call(
        add_again_kernel,
        grid_spec=pltpu.PrefetchScalarGridSpec(
            num_scalar_prefetch=1,
            grid=(HALF,),
            in_specs=[pl.BlockSpec((1, ROWS, N), lambda b, p: (b, 0, 0))] * 8,
            out_specs=[spec] * 2,
            scratch_shapes=[pltpu.VMEM((2, ROWS, N), F32)],
        ),
        out_shape=[jax.ShapeDtypeStruct((2, HALF, PIECE, N), F32)] * 2,
        compiler_params=pltpu.CompilerParams(dimension_semantics=("arbitrary",), vmem_limit_bytes=SMALL),
        cost_estimate=pl.CostEstimate(flops=1_000_000, bytes_accessed=3_300_000, transcendentals=0),
        name="add_again",
    )(place, *first, *second)


def pack_kernel(index_ref, keep, recv, out_ref, total):
    squares = jnp.zeros((PIECE, N), F32)
    for b in range(BLK):
        value = keep[b // HALF, b % HALF] + recv[b // HALF, b % HALF]
        for c in range(4):
            total[b, pl.ds(c * PIECE, PIECE), :] = value[:, c * 128 : (c + 1) * 128]
        squares += value * value
    square = jnp.broadcast_to(jnp.sum(squares), (8, 128))

    @pl.loop(0, NDP)
    def _(o):
        for s in range(SLOTS):
            out_ref[o, pl.ds(s * CHUNK, CHUNK), :] = total[index_ref[s, o]]
        out_ref[o, pl.ds(SLOTS * CHUNK, 8), :] = square


def pack(index, keep, recv):
    return pl.pallas_call(
        pack_kernel,
        in_specs=[pl.BlockSpec(memory_space=pltpu.SMEM)] + [pl.BlockSpec(memory_space=pltpu.VMEM)] * 2,
        out_specs=pl.BlockSpec(memory_space=pltpu.VMEM),
        out_shape=jax.ShapeDtypeStruct((NDP, MESSAGE, 128), F32),
        scratch_shapes=[pltpu.VMEM((BLK, CHUNK, 128), F32)],
        compiler_params=pltpu.CompilerParams(vmem_limit_bytes=SMALL),
        cost_estimate=pl.CostEstimate(flops=300_000, bytes_accessed=3_000_000, transcendentals=0),
        name="pack",
    )(index, keep, recv)


def unpack(full, ref, offset, scale):
    for source in range(NDP):
        for c in range(4):
            piece = ref[source, pl.ds(offset + c * PIECE, PIECE), :]
            full[pl.ds(piece_row(source), PIECE), pl.ds(c * 128, 128)] = piece * scale


def clip_of(sums):
    total = (sums[0][...] + sums[1][...]) + (sums[2][...] + sums[3][...])
    return (1.0 / jnp.sqrt(total / ENTRIES + tiny_offset))[0:1, 0:1]


def piece_row(device):
    return (device % 4) * 128 + (device // 4 % 4) * ROWS + (device // 16) * PIECE


def task_kernel(occ, s0, s1, s2, s3, own_g, own_old, other_g, other_old, own_dir, other_dir, g2, gt2, full, whole, old, norms, sem, *pairs):
    m, f, p, q, m1, f1, x = (pairs[2 * k : 2 * k + 2] for k in range(7))
    task = pl.program_id(0)

    def halves_to(ref):
        return lambda i, j, acc: store_block(ref, i, j, acc)

    def factor(i, j, moving):
        return scaled_eye(1.25) - 0.25 * moving if i == j else -0.25 * moving

    @pl.when(occ[task] > 0)
    def _():
        clip = clip_of((s0, s1, s2, s3))

        @pl.when(task == 0)
        def _():
            pltpu.make_async_copy(other_old.at[0, 0, 0], old, sem).start()
            unpack(full, other_g, 0, clip)

        @pl.when(task == 1)
        def _():
            pltpu.make_async_copy(own_old.at[0, 0, 0], old, sem).start()
            unpack(full, own_g, 0, clip)

        g = full[...]
        squares = jnp.sum(g * g)
        store(g2, pl.ds(0, N), g)
        store(gt2, pl.ds(0, N), g.T)

        def gram(side, a, b):
            def finish(i, j, acc):
                whole[side, *area(i, j)] = (1.0 - decay_rate) * acc + (scaled_eye(ridge_term) if i == j else 0.0)

            symmetric(a, b, finish)

        gram(0, g2, gt2)
        gram(1, gt2, g2)
        pltpu.make_async_copy(own_old.at[0, 0, 0], old, sem).wait()
        sides = (0, 1)
        for side in sides:
            mixed = whole[side] + decay_rate * old[side]
            whole[side] = mixed
            norm2 = jnp.sum(mixed * mixed)
            norms[side] = norm2
            inverse = (1.0 / jnp.sqrt(jnp.full((8, 128), norm2, F32)))[0:1, 0:1]
            for i in range(2):
                for j in range(2):
                    moving = whole[side, *area(i, j)] * inverse
                    store_block(m[side], i, j, moving)
                    store_block(f[side], i, j, factor(i, j, moving))

        def moved(to, factor_to):
            def finish(i, j, acc):
                if to is not None:
                    store_block(to, i, j, acc)
                store_block(factor_to, i, j, factor(i, j, acc))

            return finish

        for side in sides:
            symmetric(f[side], f[side], halves_to(p[side]))
        for side in sides:
            symmetric(p[side], p[side], halves_to(q[side]))
        for side in sides:
            symmetric(q[side], m[side], moved(m1[side], f1[side]))
        for side in sides:
            symmetric(f1[side], f1[side], halves_to(p[side]))
        for side in sides:
            symmetric(f[side], f1[side], halves_to(x[side]))
        for side in sides:
            symmetric(p[side], p[side], halves_to(q[side]))
        for side in sides:
            symmetric(q[side], m1[side], moved(None, m[side]))
        for side in sides:
            symmetric(x[side], m[side], halves_to(f[side]))

        def last(r, rows, acc):
            full[rows, :] = acc

        product(f[0], g2, lambda r, rows, acc: store(p[0], rows, acc))
        product(p[0], f[1], last)
        precond = full[...] * (power_eighth(norms[0]) * power_eighth(norms[1]))
        entries = N * N
        actual = jnp.full((8, 128), jnp.sum(precond * precond) / entries + tiny_offset, F32)
        target = jnp.full((8, 128), squares / entries + tiny_offset, F32)
        graft = (jnp.sqrt(target) / jnp.sqrt(actual))[0:1, 0:1]
        full[...] = precond * graft

        @pl.when(task == 0)
        def _():
            for device in range(NDP):
                other_dir[device, 0] = full[pl.ds(piece_row(device), PIECE), :].astype(BF)

        @pl.when(task == 1)
        def _():
            for device in range(NDP):
                own_dir[device, 0] = full[pl.ds(piece_row(device), PIECE), :].astype(BF)


def pair():
    return pltpu.VMEM((2, N, N), BF)


def run_tasks(occupied, sums, own_g, own_pairs, other_g, other_pair):
    result = jax.ShapeDtypeStruct((NDP, 1, PIECE, N), BF)
    return pl.pallas_call(
        task_kernel,
        grid=(2,),
        in_specs=[pl.BlockSpec(memory_space=pltpu.SMEM)]
        + [pl.BlockSpec(memory_space=pltpu.VMEM)] * 4
        + [pl.BlockSpec(memory_space=space) for space in (pltpu.VMEM, pltpu.HBM, pltpu.VMEM, pltpu.HBM)],
        out_specs=[pl.BlockSpec(memory_space=pltpu.VMEM)] * 2,
        out_shape=[result, result],
        scratch_shapes=[pair(), pair(), pltpu.VMEM((N, N), F32)]
        + [pltpu.VMEM((2, N, N), F32), pltpu.VMEM((2, N, N), F32), pltpu.SMEM((2,), F32), pltpu.SemaphoreType.DMA]
        + [pair() for _ in range(14)],
        compiler_params=pltpu.CompilerParams(dimension_semantics=("arbitrary",), vmem_limit_bytes=36 << 20),
        cost_estimate=pl.CostEstimate(flops=16_000_000_000, bytes_accessed=3_500_000, transcendentals=0),
        name="tasks",
    )(occupied, *sums, own_g, pltpu.with_memory_space_constraint(own_pairs, pltpu.HBM), other_g, other_pair)


def state_kernel(occ, s0, s1, s2, s3, g_ref, old_ref, new_ref, full, g2, gt2):
    s = pl.program_id(0)

    @pl.when(occ[s] > 0)
    def _():
        unpack(full, g_ref, pl.multiple_of(s * CHUNK, CHUNK), clip_of((s0, s1, s2, s3)))
        g = full[...]
        store(g2, pl.ds(0, N), g)
        store(gt2, pl.ds(0, N), g.T)

        def mix(side):
            def finish(r, rows, acc):
                new_ref[0, 0, 0, side, rows, :] = (
                    decay_rate * old_ref[0, 0, 0, side, rows, :] + (1.0 - decay_rate) * acc
                )

            return finish

        product(g2, gt2, mix(0))
        product(gt2, g2, mix(1))

    @pl.when(occ[s] <= 0)
    def _():
        new_ref[...] = old_ref[...]


def new_state(occupied, sums, gathered, pairs):
    block = pl.BlockSpec((1, 1, 1, 2, N, N), lambda s: (0, 0, s, 0, 0, 0))
    return pl.pallas_call(
        state_kernel,
        grid=(SLOTS,),
        in_specs=[
            pl.BlockSpec(memory_space=pltpu.SMEM),
        ]
        + [pl.BlockSpec(memory_space=pltpu.VMEM)] * 5
        + [block],
        out_specs=block,
        out_shape=jax.ShapeDtypeStruct(pairs.shape, F32),
        scratch_shapes=[pltpu.VMEM((N, N), F32), pair(), pair()],
        compiler_params=pltpu.CompilerParams(dimension_semantics=("arbitrary",), vmem_limit_bytes=SMALL),
        cost_estimate=pl.CostEstimate(flops=3_000_000_000, bytes_accessed=10_000_000, transcendentals=0),
        name="state",
    )(occupied, *sums, gathered, pairs)


def pick_kernel(owner, slot, recv_ref, out_ref):
    for b in range(BLK):
        out_ref[b] = recv_ref[owner[b], slot[b]]


def pick(owner, slot, recv):
    return pl.pallas_call(
        pick_kernel,
        in_specs=[pl.BlockSpec(memory_space=pltpu.SMEM)] * 2 + [pl.BlockSpec(memory_space=pltpu.VMEM)],
        out_specs=pl.BlockSpec(memory_space=pltpu.VMEM),
        out_shape=jax.ShapeDtypeStruct((BLK, PIECE, N), BF),
        compiler_params=pltpu.CompilerParams(vmem_limit_bytes=SMALL),
        name="pick",
    )(owner, slot, recv)


def place_kernel(steps, place, *refs):
    count = 2 * len(steps)
    groups, out, sems = (refs[: len(steps)], refs[len(steps) : count]), refs[-2], refs[-1]
    x, y, z = place[0], place[1], place[2]
    copies = []
    for number, (far, low) in enumerate(steps):
        for near in range(2) if far == 2 else range(4):
            for dz in range(2):
                for group in range(2):
                    dx, dy = (far, near + low) if group == 0 else (near + low, far)
                    row = lax.rem(z + dz, 2) * PIECE + lax.rem(y + 4 - dy, 4) * ROWS + lax.rem(x + 4 - dx, 4) * 128
                    copies.append(
                        pltpu.make_async_copy(
                            groups[group][number].at[near, dz],
                            out.at[pl.ds(group * HALF, HALF), pl.ds(pl.multiple_of(row, PIECE), PIECE), :],
                            sems.at[len(copies)],
                        )
                    )
    for copy in copies:
        copy.start()
    for copy in copies:
        copy.wait()


def place_some(place, first, second, steps, placed):
    refs = [*first, *second] + ([] if placed is None else [placed])
    return pl.pallas_call(
        functools.partial(place_kernel, steps),
        in_specs=[pl.BlockSpec(memory_space=pltpu.SMEM)]
        + [pl.BlockSpec(memory_space=pltpu.VMEM)] * (2 * len(steps))
        + ([] if placed is None else [pl.BlockSpec(memory_space=pl.ANY)]),
        out_specs=pl.BlockSpec(memory_space=pl.ANY),
        out_shape=jax.ShapeDtypeStruct((BLK, N, N), BF),
        scratch_shapes=[pltpu.SemaphoreType.DMA((48 if placed is None else 16,))],
        input_output_aliases={} if placed is None else {len(refs): 0},
        compiler_params=pltpu.CompilerParams(vmem_limit_bytes=SMALL),
        cost_estimate=pl.CostEstimate(flops=0, bytes_accessed=8_000_000, transcendentals=0),
        name="place" if placed is None else "place_last",
    )(place, *refs)


def place_all(place, first, second):
    near = place_some(place, first[:3], second[:3], ((0, 0), (1, 0), (3, 0)), None)
    return place_some(place, first[3:], second[3:], ((2, 0), (2, 2)), near)


def spread(v, dx, dy, dz):
    steps = 2 if dz else 4
    return [v] + [lax.ppermute(v, "dp", dp_pairs(dx * k, dy * k, dz * k)) for k in range(1, steps)]


def around(v, dx, dy):
    ahead, behind = dp_pairs(dx, dy, 0), dp_pairs(3 * dx, 3 * dy, 0)
    back = lax.ppermute(v, "dp", ahead)
    front = lax.ppermute(v, "dp", behind)
    return [v, back, front, lax.ppermute(back[:2], "dp", ahead), lax.ppermute(front[2:], "dp", behind)]


def spread(v, dx, dy, dz):
    steps = 2 if dz else 4
    return [v] + [lax.ppermute(v, "dp", dp_pairs(dx * k, dy * k, dz * k)) for k in range(1, steps)]


def owner_slots(owners):
    positions = jnp.arange(owners.shape[0], dtype=jnp.int32)
    same_owner = owners[:, None] == owners[None, :]
    earlier = positions[None, :] < positions[:, None]
    return jnp.sum((same_owner & earlier).astype(jnp.int32), axis=1)


def shards(gradients, factor_state, block_owner):
    owners = block_owner[0]
    myself = lax.axis_index("dp")
    slot_of = owner_slots(owners)
    positions = jnp.arange(BLK, dtype=jnp.int32)
    slots = jnp.arange(SLOTS, dtype=jnp.int32)
    devices = jnp.arange(NDP, dtype=jnp.int32)
    match = (owners == devices[None, :, None]) & (slot_of == slots[:, None, None])
    index = jnp.sum(jnp.where(match, positions, 0), axis=2)
    mine = (owners == myself) & (slot_of == slots[:, None])
    occupied = jnp.max(mine.astype(jnp.int32), axis=1)
    other_occupied = lax.ppermute(occupied[1:2], "mp", CORE_PAIRS)
    other_pair = lax.ppermute(factor_state[:, :, 1:2], "mp", CORE_PAIRS)

    place = jnp.stack([myself % 4, (myself // 4) % 4, myself // 16]).astype(jnp.int32)
    grads = gradients[0].reshape(BLK, 4, 4, ROWS, N)
    pieces = cut(place, grads)
    grads, pieces = lax.optimization_barrier((grads, pieces))
    first, second = [None] * 4, [None] * 4
    for k in (1, 3, 2):
        first[k] = lax.ppermute(pieces[k - 1], "dp", dp_pairs(k, 0, 0))
        second[k] = lax.ppermute(pieces[k + 2], "dp", dp_pairs(0, k, 0))
    zero = jnp.int32(0)
    start = (zero, place[0], zero, zero, zero)
    first[0] = lax.dynamic_slice(grads, start, (HALF, 1, 4, ROWS, N)).reshape(HALF, 4, ROWS, N)
    start = (jnp.int32(HALF), zero, place[1], zero, zero)
    second[0] = lax.dynamic_slice(grads, start, (HALF, 4, 1, ROWS, N)).reshape(HALF, 4, ROWS, N)
    first = list(add_pieces(place, first, 1))
    second = list(add_pieces(place, second, 0))
    for k in (1, 3, 2):
        first[k] = lax.ppermute(first[k], "dp", dp_pairs(0, k, 0))
        second[k] = lax.ppermute(second[k], "dp", dp_pairs(k, 0, 0))
    keep, send = add_again(place, first, second)
    tasks = jnp.concatenate([other_occupied, occupied[0:1]])
    index, tasks, occupied = lax.optimization_barrier((index, tasks, occupied))
    packed = pack(index, keep, lax.ppermute(send, "dp", dp_pairs(0, 0, 1)))
    gathered = lax.all_to_all(packed, "dp", split_axis=0, concat_axis=0, tiled=True)
    other = lax.ppermute(gathered[:, CHUNK : 2 * CHUNK], "mp", CORE_PAIRS)
    squares = jnp.sum(gathered[:, SLOTS * CHUNK :], axis=0)
    sums = [squares] + [lax.ppermute(squares, "mp", [(i, i ^ bit) for i in range(4)]) for bit in (1, 2, 3)]
    own, helped = run_tasks(tasks, sums, gathered, factor_state, other, other_pair)
    returned = lax.ppermute(helped, "mp", CORE_PAIRS)
    outgoing = jnp.concatenate([own, returned], axis=1)
    incoming = lax.all_to_all(outgoing, "dp", split_axis=0, concat_axis=0, tiled=True)
    piece = pick(owners, slot_of, incoming)

    column = jnp.stack(spread(piece, 0, 0, 1))
    first = jnp.stack(spread(column[:, :HALF], 0, 1, 0))
    second = jnp.stack(spread(column[:, HALF:], 1, 0, 0))
    first = around(first, 1, 0)
    second = around(second, 0, 1)
    directions = place_all(place, first, second)
    next_state = new_state(occupied, sums, gathered, factor_state)
    return directions, next_state


def solution(mesh):
    in_specs = (P("dp", "mp", None, None), P("mp", "dp", None, None, None, None), P("mp", None))
    out_specs = (P("mp", None, None), P("mp", "dp", None, None, None, None))
    return jax.shard_map(shards, mesh=mesh, in_specs=in_specs, out_specs=out_specs, check_vma=False)
```

```python
import functools

import jax
import jax.numpy as jnp
from jax import lax
from jax.experimental import pallas as pl
from jax.experimental.pallas import tpu as pltpu
from jax.sharding import PartitionSpec as P

SLOTS = 2
N = 512
BLK = 10
NDP = 32
PIECE = N // NDP
ROWS = 2 * PIECE
CHUNK = PIECE * N // 128
MESSAGE = SLOTS * CHUNK + 8
ENTRIES = N * N * BLK * 4
HALF = BLK // 2
TR = 256
SMALL = 16 << 20
F32 = jnp.float32
BF = jnp.bfloat16

decay_rate = 0.95
ridge_term = 0.001
tiny_offset = 1e-06


def dp_pairs(dx, dy, dz):
    pairs = []
    for z in range(2):
        for y in range(4):
            for x in range(4):
                to = ((z + dz) % 2) * 16 + ((y + dy) % 4) * 4 + (x + dx) % 4
                pairs.append((z * 16 + y * 4 + x, to))
    return pairs


CORE_PAIRS = [(0, 1), (1, 0), (2, 3), (3, 2)]


def split(v):
    hi = v.astype(BF)
    return hi, (v - hi.astype(F32)).astype(BF)


def dot(a, b):
    return jnp.dot(a, b, preferred_element_type=F32)


def scaled_eye(value):
    i = lax.broadcasted_iota(jnp.int32, (TR, TR), 0)
    j = lax.broadcasted_iota(jnp.int32, (TR, TR), 1)
    return jnp.where(i == j, value, 0.0)


def store(ref, rows, v):
    hi, lo = split(v)
    ref[0, rows, :] = hi
    ref[1, rows, :] = lo


def area(i, j):
    return pl.ds(i * TR, TR), pl.ds(j * TR, TR)


def store_block(ref, i, j, v):
    rows, columns = area(i, j)
    hi, lo = split(v)
    ref[0, rows, columns] = hi
    ref[1, rows, columns] = lo


def product(a, b, finish):
    for r in range(N // TR):
        rows = pl.ds(r * TR, TR)
        ah = a[0, rows, :]
        al = a[1, rows, :]
        finish(r, rows, dot(ah, b[0]) + (dot(ah, b[1]) + dot(al, b[0])))


def symmetric(a, b, finish):
    top = pl.ds(0, TR)
    low = pl.ds(TR, TR)
    ah = a[0, top, :]
    al = a[1, top, :]
    acc = dot(ah, b[0]) + (dot(ah, b[1]) + dot(al, b[0]))
    finish(0, 0, acc[:, :TR])
    side = acc[:, TR:]
    finish(0, 1, side)
    finish(1, 0, side.T)
    ah = a[0, low, :]
    al = a[1, low, :]
    finish(1, 1, dot(ah, b[0, :, low]) + (dot(ah, b[1, :, low]) + dot(al, b[0, :, low])))


def power_eighth(total):
    wide = jnp.full((8, 128), total, F32)
    return (1.0 / jnp.sqrt(jnp.sqrt(jnp.sqrt(wide))))[0:1, 0:1]


def cut_kernel(place, grads, *refs):
    outs, held, ins, puts = refs[:6], refs[6], refs[7], refs[8]
    gets = []
    for k in (1, 3, 2):
        x = lax.rem(place[0] + k, 4)
        y = lax.rem(place[1] + k, 4)
        gets.append((k - 1, grads.at[pl.ds(0, HALF), x]))
        gets.append((k + 2, grads.at[pl.ds(HALF, HALF), :, y]))
    copies = [(n, pltpu.make_async_copy(source, held.at[n], ins.at[n])) for n, source in gets]
    for _, copy in copies:
        copy.start()
    stores = []
    for n, copy in copies:
        copy.wait()
        stores.append(pltpu.make_async_copy(held.at[n], outs[n], puts.at[n]))
        stores[-1].start()
    for copy in stores:
        copy.wait()


def cut(place, grads):
    return pl.pallas_call(
        cut_kernel,
        in_specs=[pl.BlockSpec(memory_space=pltpu.SMEM), pl.BlockSpec(memory_space=pltpu.HBM)],
        out_specs=[pl.BlockSpec(memory_space=pl.ANY)] * 6,
        out_shape=[jax.ShapeDtypeStruct((HALF, 4, ROWS, N), BF)] * 6,
        scratch_shapes=[
            pltpu.VMEM((6, HALF, 4, ROWS, N), BF),
            pltpu.SemaphoreType.DMA((6,)),
            pltpu.SemaphoreType.DMA((6,)),
        ],
        compiler_params=pltpu.CompilerParams(vmem_limit_bytes=SMALL),
        name="cut",
    )(place, pltpu.with_memory_space_constraint(grads, pltpu.HBM))


def add_kernel(across, place, own, r1, r2, r3, *outs):
    here = place[across]

    @pl.loop(0, HALF)
    def _(b):
        for step, out in enumerate(outs):
            j = lax.rem(here + step, 4)
            out[b] = (own[b, j].astype(F32) + r1[b, j].astype(F32)) + (r2[b, j].astype(F32) + r3[b, j].astype(F32))


def add_pieces(place, pieces, across):
    return pl.pallas_call(
        functools.partial(add_kernel, across),
        in_specs=[pl.BlockSpec(memory_space=pltpu.SMEM)] + [pl.BlockSpec(memory_space=pltpu.VMEM)] * 4,
        out_specs=[pl.BlockSpec(memory_space=pltpu.VMEM)] * 4,
        out_shape=[jax.ShapeDtypeStruct((HALF, ROWS, N), F32)] * 4,
        compiler_params=pltpu.CompilerParams(vmem_limit_bytes=SMALL),
        cost_estimate=pl.CostEstimate(flops=2_000_000, bytes_accessed=4_000_000, transcendentals=0),
    )(place, *pieces)


def add_again_kernel(place, *refs):
    keep, send, total = refs[8], refs[9], refs[10]
    for group in range(2):
        a, b, c, d = (ref[0] for ref in refs[4 * group : 4 * group + 4])
        total[group] = (a + b) + (c + d)
    z = place[2]
    near = pl.multiple_of(z * PIECE, PIECE)
    far = pl.multiple_of((1 - z) * PIECE, PIECE)
    keep[:, 0] = total[:, pl.ds(near, PIECE), :]
    send[:, 0] = total[:, pl.ds(far, PIECE), :]


def add_again(place, first, second):
    spec = pl.BlockSpec((2, 1, PIECE, N), lambda b, p: (0, b, 0, 0))
    return pl.pallas_call(
        add_again_kernel,
        grid_spec=pltpu.PrefetchScalarGridSpec(
            num_scalar_prefetch=1,
            grid=(HALF,),
            in_specs=[pl.BlockSpec((1, ROWS, N), lambda b, p: (b, 0, 0))] * 8,
            out_specs=[spec] * 2,
            scratch_shapes=[pltpu.VMEM((2, ROWS, N), F32)],
        ),
        out_shape=[jax.ShapeDtypeStruct((2, HALF, PIECE, N), F32)] * 2,
        compiler_params=pltpu.CompilerParams(dimension_semantics=("arbitrary",), vmem_limit_bytes=SMALL),
        cost_estimate=pl.CostEstimate(flops=1_000_000, bytes_accessed=3_300_000, transcendentals=0),
        name="add_again",
    )(place, *first, *second)


def pack_kernel(index_ref, keep, recv, out_ref, total):
    squares = jnp.zeros((PIECE, N), F32)
    for b in range(BLK):
        value = keep[b // HALF, b % HALF] + recv[b // HALF, b % HALF]
        for c in range(4):
            total[b, pl.ds(c * PIECE, PIECE), :] = value[:, c * 128 : (c + 1) * 128]
        squares += value * value
    square = jnp.broadcast_to(jnp.sum(squares), (8, 128))

    @pl.loop(0, NDP)
    def _(o):
        for s in range(SLOTS):
            out_ref[o, pl.ds(s * CHUNK, CHUNK), :] = total[index_ref[s, o]]
        out_ref[o, pl.ds(SLOTS * CHUNK, 8), :] = square


def pack(index, keep, recv):
    return pl.pallas_call(
        pack_kernel,
        in_specs=[pl.BlockSpec(memory_space=pltpu.SMEM)] + [pl.BlockSpec(memory_space=pltpu.VMEM)] * 2,
        out_specs=pl.BlockSpec(memory_space=pltpu.VMEM),
        out_shape=jax.ShapeDtypeStruct((NDP, MESSAGE, 128), F32),
        scratch_shapes=[pltpu.VMEM((BLK, CHUNK, 128), F32)],
        compiler_params=pltpu.CompilerParams(vmem_limit_bytes=SMALL),
        cost_estimate=pl.CostEstimate(flops=300_000, bytes_accessed=3_000_000, transcendentals=0),
        name="pack",
    )(index, keep, recv)


def unpack(full, ref, offset, scale):
    for source in range(NDP):
        for c in range(4):
            piece = ref[source, pl.ds(offset + c * PIECE, PIECE), :]
            full[pl.ds(piece_row(source), PIECE), pl.ds(c * 128, 128)] = piece * scale


def clip_of(sums):
    total = (sums[0][...] + sums[1][...]) + (sums[2][...] + sums[3][...])
    return (1.0 / jnp.sqrt(total / ENTRIES + tiny_offset))[0:1, 0:1]


def piece_row(device):
    return (device % 4) * 128 + (device // 4 % 4) * ROWS + (device // 16) * PIECE


def task_kernel(occ, s0, s1, s2, s3, own_g, own_old, other_g, other_old, own_dir, other_dir, g2, gt2, full, whole, old, norms, sem, *pairs):
    m, f, p, q, m1, f1, x = (pairs[2 * k : 2 * k + 2] for k in range(7))
    task = pl.program_id(0)

    def halves_to(ref):
        return lambda i, j, acc: store_block(ref, i, j, acc)

    def factor(i, j, moving):
        return scaled_eye(1.25) - 0.25 * moving if i == j else -0.25 * moving

    @pl.when(occ[task] > 0)
    def _():
        clip = clip_of((s0, s1, s2, s3))

        @pl.when(task == 0)
        def _():
            pltpu.make_async_copy(other_old.at[0, 0, 0], old, sem).start()
            unpack(full, other_g, 0, clip)

        @pl.when(task == 1)
        def _():
            pltpu.make_async_copy(own_old.at[0, 0, 0], old, sem).start()
            unpack(full, own_g, 0, clip)

        g = full[...]
        squares = jnp.sum(g * g)
        store(g2, pl.ds(0, N), g)
        store(gt2, pl.ds(0, N), g.T)

        def gram(side, a, b):
            def finish(i, j, acc):
                whole[side, *area(i, j)] = (1.0 - decay_rate) * acc + (scaled_eye(ridge_term) if i == j else 0.0)

            symmetric(a, b, finish)

        gram(0, g2, gt2)
        gram(1, gt2, g2)
        pltpu.make_async_copy(own_old.at[0, 0, 0], old, sem).wait()
        sides = (0, 1)
        for side in sides:
            mixed = whole[side] + decay_rate * old[side]
            whole[side] = mixed
            norm2 = jnp.sum(mixed * mixed)
            norms[side] = norm2
            inverse = (1.0 / jnp.sqrt(jnp.full((8, 128), norm2, F32)))[0:1, 0:1]
            for i in range(2):
                for j in range(2):
                    moving = whole[side, *area(i, j)] * inverse
                    store_block(m[side], i, j, moving)
                    store_block(f[side], i, j, factor(i, j, moving))

        def moved(to, factor_to):
            def finish(i, j, acc):
                if to is not None:
                    store_block(to, i, j, acc)
                store_block(factor_to, i, j, factor(i, j, acc))

            return finish

        for side in sides:
            symmetric(f[side], f[side], halves_to(p[side]))
        for side in sides:
            symmetric(p[side], p[side], halves_to(q[side]))
        for side in sides:
            symmetric(q[side], m[side], moved(m1[side], f1[side]))
        for side in sides:
            symmetric(f1[side], f1[side], halves_to(p[side]))
        for side in sides:
            symmetric(f[side], f1[side], halves_to(x[side]))
        for side in sides:
            symmetric(p[side], p[side], halves_to(q[side]))
        for side in sides:
            symmetric(q[side], m1[side], moved(None, m[side]))
        for side in sides:
            symmetric(x[side], m[side], halves_to(f[side]))

        def last(r, rows, acc):
            full[rows, :] = acc

        product(f[0], g2, lambda r, rows, acc: store(p[0], rows, acc))
        product(p[0], f[1], last)
        precond = full[...] * (power_eighth(norms[0]) * power_eighth(norms[1]))
        entries = N * N
        actual = jnp.full((8, 128), jnp.sum(precond * precond) / entries + tiny_offset, F32)
        target = jnp.full((8, 128), squares / entries + tiny_offset, F32)
        graft = (jnp.sqrt(target) / jnp.sqrt(actual))[0:1, 0:1]
        full[...] = precond * graft

        @pl.when(task == 0)
        def _():
            for device in range(NDP):
                other_dir[device, 0] = full[pl.ds(piece_row(device), PIECE), :].astype(BF)

        @pl.when(task == 1)
        def _():
            for device in range(NDP):
                own_dir[device, 0] = full[pl.ds(piece_row(device), PIECE), :].astype(BF)


def pair():
    return pltpu.VMEM((2, N, N), BF)


def run_tasks(occupied, sums, own_g, own_pairs, other_g, other_pair):
    result = jax.ShapeDtypeStruct((NDP, 1, PIECE, N), BF)
    return pl.pallas_call(
        task_kernel,
        grid=(2,),
        in_specs=[pl.BlockSpec(memory_space=pltpu.SMEM)]
        + [pl.BlockSpec(memory_space=pltpu.VMEM)] * 4
        + [pl.BlockSpec(memory_space=space) for space in (pltpu.VMEM, pltpu.HBM, pltpu.VMEM, pltpu.HBM)],
        out_specs=[pl.BlockSpec(memory_space=pltpu.VMEM)] * 2,
        out_shape=[result, result],
        scratch_shapes=[pair(), pair(), pltpu.VMEM((N, N), F32)]
        + [pltpu.VMEM((2, N, N), F32), pltpu.VMEM((2, N, N), F32), pltpu.SMEM((2,), F32), pltpu.SemaphoreType.DMA]
        + [pair() for _ in range(14)],
        compiler_params=pltpu.CompilerParams(dimension_semantics=("arbitrary",), vmem_limit_bytes=36 << 20),
        cost_estimate=pl.CostEstimate(flops=16_000_000_000, bytes_accessed=3_500_000, transcendentals=0),
        name="tasks",
    )(occupied, *sums, own_g, pltpu.with_memory_space_constraint(own_pairs, pltpu.HBM), other_g, other_pair)


def state_kernel(occ, s0, s1, s2, s3, g_ref, old_ref, new_ref, full, g2, gt2):
    s = pl.program_id(0)

    @pl.when(occ[s] > 0)
    def _():
        unpack(full, g_ref, pl.multiple_of(s * CHUNK, CHUNK), clip_of((s0, s1, s2, s3)))
        g = full[...]
        store(g2, pl.ds(0, N), g)
        store(gt2, pl.ds(0, N), g.T)

        def mix(side):
            def finish(r, rows, acc):
                new_ref[0, 0, 0, side, rows, :] = (
                    decay_rate * old_ref[0, 0, 0, side, rows, :] + (1.0 - decay_rate) * acc
                )

            return finish

        product(g2, gt2, mix(0))
        product(gt2, g2, mix(1))

    @pl.when(occ[s] <= 0)
    def _():
        new_ref[...] = old_ref[...]


def new_state(occupied, sums, gathered, pairs):
    block = pl.BlockSpec((1, 1, 1, 2, N, N), lambda s: (0, 0, s, 0, 0, 0))
    return pl.pallas_call(
        state_kernel,
        grid=(SLOTS,),
        in_specs=[
            pl.BlockSpec(memory_space=pltpu.SMEM),
        ]
        + [pl.BlockSpec(memory_space=pltpu.VMEM)] * 5
        + [block],
        out_specs=block,
        out_shape=jax.ShapeDtypeStruct(pairs.shape, F32),
        scratch_shapes=[pltpu.VMEM((N, N), F32), pair(), pair()],
        compiler_params=pltpu.CompilerParams(dimension_semantics=("arbitrary",), vmem_limit_bytes=SMALL),
        cost_estimate=pl.CostEstimate(flops=3_000_000_000, bytes_accessed=10_000_000, transcendentals=0),
        name="state",
    )(occupied, *sums, gathered, pairs)


def pick_kernel(owner, slot, recv_ref, out_ref):
    for b in range(BLK):
        out_ref[b] = recv_ref[owner[b], slot[b]]


def pick(owner, slot, recv):
    return pl.pallas_call(
        pick_kernel,
        in_specs=[pl.BlockSpec(memory_space=pltpu.SMEM)] * 2 + [pl.BlockSpec(memory_space=pltpu.VMEM)],
        out_specs=pl.BlockSpec(memory_space=pltpu.VMEM),
        out_shape=jax.ShapeDtypeStruct((BLK, PIECE, N), BF),
        compiler_params=pltpu.CompilerParams(vmem_limit_bytes=SMALL),
        name="pick",
    )(owner, slot, recv)


def place_kernel(steps, place, *refs):
    count = 2 * len(steps)
    groups, out, sems = (refs[: len(steps)], refs[len(steps) : count]), refs[-2], refs[-1]
    x, y, z = place[0], place[1], place[2]
    copies = []
    for number, (far, low) in enumerate(steps):
        for near in range(2) if far == 2 else range(4):
            for dz in range(2):
                for group in range(2):
                    dx, dy = (far, near + low) if group == 0 else (near + low, far)
                    row = lax.rem(z + dz, 2) * PIECE + lax.rem(y + 4 - dy, 4) * ROWS + lax.rem(x + 4 - dx, 4) * 128
                    copies.append(
                        pltpu.make_async_copy(
                            groups[group][number].at[near, dz],
                            out.at[pl.ds(group * HALF, HALF), pl.ds(pl.multiple_of(row, PIECE), PIECE), :],
                            sems.at[len(copies)],
                        )
                    )
    for copy in copies:
        copy.start()
    for copy in copies:
        copy.wait()


def place_some(place, first, second, steps, placed):
    refs = [*first, *second] + ([] if placed is None else [placed])
    return pl.pallas_call(
        functools.partial(place_kernel, steps),
        in_specs=[pl.BlockSpec(memory_space=pltpu.SMEM)]
        + [pl.BlockSpec(memory_space=pltpu.VMEM)] * (2 * len(steps))
        + ([] if placed is None else [pl.BlockSpec(memory_space=pl.ANY)]),
        out_specs=pl.BlockSpec(memory_space=pl.ANY),
        out_shape=jax.ShapeDtypeStruct((BLK, N, N), BF),
        scratch_shapes=[pltpu.SemaphoreType.DMA((48 if placed is None else 16,))],
        input_output_aliases={} if placed is None else {len(refs): 0},
        compiler_params=pltpu.CompilerParams(vmem_limit_bytes=SMALL),
        cost_estimate=pl.CostEstimate(flops=0, bytes_accessed=8_000_000, transcendentals=0),
        name="place" if placed is None else "place_last",
    )(place, *refs)


def place_all(place, first, second):
    near = place_some(place, first[:3], second[:3], ((0, 0), (1, 0), (3, 0)), None)
    return place_some(place, first[3:], second[3:], ((2, 0), (2, 2)), near)


def spread(v, dx, dy, dz):
    steps = 2 if dz else 4
    return [v] + [lax.ppermute(v, "dp", dp_pairs(dx * k, dy * k, dz * k)) for k in range(1, steps)]


def around(v, dx, dy):
    ahead, behind = dp_pairs(dx, dy, 0), dp_pairs(3 * dx, 3 * dy, 0)
    back = lax.ppermute(v, "dp", ahead)
    front = lax.ppermute(v, "dp", behind)
    return [v, back, front, lax.ppermute(back[:2], "dp", ahead), lax.ppermute(front[2:], "dp", behind)]


def spread(v, dx, dy, dz):
    steps = 2 if dz else 4
    return [v] + [lax.ppermute(v, "dp", dp_pairs(dx * k, dy * k, dz * k)) for k in range(1, steps)]


def owner_slots(owners):
    positions = jnp.arange(owners.shape[0], dtype=jnp.int32)
    same_owner = owners[:, None] == owners[None, :]
    earlier = positions[None, :] < positions[:, None]
    return jnp.sum((same_owner & earlier).astype(jnp.int32), axis=1)


def shards(gradients, factor_state, block_owner):
    owners = block_owner[0]
    myself = lax.axis_index("dp")
    slot_of = owner_slots(owners)
    positions = jnp.arange(BLK, dtype=jnp.int32)
    slots = jnp.arange(SLOTS, dtype=jnp.int32)
    devices = jnp.arange(NDP, dtype=jnp.int32)
    match = (owners == devices[None, :, None]) & (slot_of == slots[:, None, None])
    index = jnp.sum(jnp.where(match, positions, 0), axis=2)
    mine = (owners == myself) & (slot_of == slots[:, None])
    occupied = jnp.max(mine.astype(jnp.int32), axis=1)
    other_occupied = lax.ppermute(occupied[1:2], "mp", CORE_PAIRS)
    other_pair = lax.ppermute(factor_state[:, :, 1:2], "mp", CORE_PAIRS)

    place = jnp.stack([myself % 4, (myself // 4) % 4, myself // 16]).astype(jnp.int32)
    grads = gradients[0].reshape(BLK, 4, 4, ROWS, N)
    pieces = cut(place, grads)
    grads, pieces = lax.optimization_barrier((grads, pieces))
    first, second = [None] * 4, [None] * 4
    for k in (1, 3, 2):
        first[k] = lax.ppermute(pieces[k - 1], "dp", dp_pairs(k, 0, 0))
        second[k] = lax.ppermute(pieces[k + 2], "dp", dp_pairs(0, k, 0))
    zero = jnp.int32(0)
    start = (zero, place[0], zero, zero, zero)
    first[0] = lax.dynamic_slice(grads, start, (HALF, 1, 4, ROWS, N)).reshape(HALF, 4, ROWS, N)
    start = (jnp.int32(HALF), zero, place[1], zero, zero)
    second[0] = lax.dynamic_slice(grads, start, (HALF, 4, 1, ROWS, N)).reshape(HALF, 4, ROWS, N)
    first = list(add_pieces(place, first, 1))
    second = list(add_pieces(place, second, 0))
    for k in (1, 3, 2):
        first[k] = lax.ppermute(first[k], "dp", dp_pairs(0, k, 0))
        second[k] = lax.ppermute(second[k], "dp", dp_pairs(k, 0, 0))
    keep, send = add_again(place, first, second)
    tasks = jnp.concatenate([other_occupied, occupied[0:1]])
    index, tasks, occupied = lax.optimization_barrier((index, tasks, occupied))
    packed = pack(index, keep, lax.ppermute(send, "dp", dp_pairs(0, 0, 1)))
    gathered = lax.all_to_all(packed, "dp", split_axis=0, concat_axis=0, tiled=True)
    other = lax.ppermute(gathered[:, CHUNK : 2 * CHUNK], "mp", CORE_PAIRS)
    squares = jnp.sum(gathered[:, SLOTS * CHUNK :], axis=0)
    sums = [squares] + [lax.ppermute(squares, "mp", [(i, i ^ bit) for i in range(4)]) for bit in (1, 2, 3)]
    own, helped = run_tasks(tasks, sums, gathered, factor_state, other, other_pair)
    returned = lax.ppermute(helped, "mp", CORE_PAIRS)
    outgoing = jnp.concatenate([own, returned], axis=1)
    incoming = lax.all_to_all(outgoing, "dp", split_axis=0, concat_axis=0, tiled=True)
    piece = pick(owners, slot_of, incoming)

    column = jnp.stack(spread(piece, 0, 0, 1))
    first = jnp.stack(spread(column[:, :HALF], 0, 1, 0))
    second = jnp.stack(spread(column[:, HALF:], 1, 0, 0))
    first = around(first, 1, 0)
    second = around(second, 0, 1)
    directions = place_all(place, first, second)
    next_state = new_state(occupied, sums, gathered, factor_state)
    return directions, next_state


def solution(mesh):
    in_specs = (P("dp", "mp", None, None), P("mp", "dp", None, None, None, None), P("mp", None))
    out_specs = (P("mp", None, None), P("mp", "dp", None, None, None, None))
    return jax.shard_map(shards, mesh=mesh, in_specs=in_specs, out_specs=out_specs, check_vma=False)
```

```python
import functools

import jax
import jax.numpy as jnp
from jax import lax
from jax.experimental import pallas as pl
from jax.experimental.pallas import tpu as pltpu
from jax.sharding import PartitionSpec as P

SLOTS = 2
N = 512
BLK = 10
NDP = 32
PIECE = N // NDP
ROWS = 2 * PIECE
CHUNK = PIECE * N // 128
MESSAGE = SLOTS * CHUNK + 8
ENTRIES = N * N * BLK * 4
HALF = BLK // 2
TR = 256
SMALL = 16 << 20
F32 = jnp.float32
BF = jnp.bfloat16

decay_rate = 0.95
ridge_term = 0.001
tiny_offset = 1e-06


def dp_pairs(dx, dy, dz):
    pairs = []
    for z in range(2):
        for y in range(4):
            for x in range(4):
                to = ((z + dz) % 2) * 16 + ((y + dy) % 4) * 4 + (x + dx) % 4
                pairs.append((z * 16 + y * 4 + x, to))
    return pairs


CORE_PAIRS = [(0, 1), (1, 0), (2, 3), (3, 2)]


def split(v):
    hi = v.astype(BF)
    return hi, (v - hi.astype(F32)).astype(BF)


def dot(a, b):
    return jnp.dot(a, b, preferred_element_type=F32)


def scaled_eye(value):
    i = lax.broadcasted_iota(jnp.int32, (TR, TR), 0)
    j = lax.broadcasted_iota(jnp.int32, (TR, TR), 1)
    return jnp.where(i == j, value, 0.0)


def store(ref, rows, v):
    hi, lo = split(v)
    ref[0, rows, :] = hi
    ref[1, rows, :] = lo


def area(i, j):
    return pl.ds(i * TR, TR), pl.ds(j * TR, TR)


def store_block(ref, i, j, v):
    rows, columns = area(i, j)
    hi, lo = split(v)
    ref[0, rows, columns] = hi
    ref[1, rows, columns] = lo


def three(a, rows, b, columns):
    both = dot(a[:, rows, :].reshape(2 * TR, N), b[0, :, columns])
    return both[:TR] + (dot(a[0, rows, :], b[1, :, columns]) + both[TR:])


def product(a, b, finish):
    for r in range(N // TR):
        rows = pl.ds(r * TR, TR)
        finish(r, rows, three(a, rows, b, pl.ds(0, N)))


def symmetric(a, b, finish):
    top = pl.ds(0, TR)
    low = pl.ds(TR, TR)
    acc = three(a, top, b, pl.ds(0, N))
    finish(0, 0, acc[:, :TR])
    side = acc[:, TR:]
    finish(0, 1, side)
    finish(1, 0, side.T)
    finish(1, 1, three(a, low, b, low))


def power_eighth(total):
    wide = jnp.full((8, 128), total, F32)
    return (1.0 / jnp.sqrt(jnp.sqrt(jnp.sqrt(wide))))[0:1, 0:1]


def cut_kernel(place, grads, *refs):
    outs, held, ins, puts = refs[:6], refs[6], refs[7], refs[8]
    gets = []
    for k in (1, 3, 2):
        x = lax.rem(place[0] + k, 4)
        y = lax.rem(place[1] + k, 4)
        gets.append((k - 1, grads.at[pl.ds(0, HALF), x]))
        gets.append((k + 2, grads.at[pl.ds(HALF, HALF), :, y]))
    copies = [(n, pltpu.make_async_copy(source, held.at[n], ins.at[n])) for n, source in gets]
    for _, copy in copies:
        copy.start()
    stores = []
    for n, copy in copies:
        copy.wait()
        stores.append(pltpu.make_async_copy(held.at[n], outs[n], puts.at[n]))
        stores[-1].start()
    for copy in stores:
        copy.wait()


def cut(place, grads):
    return pl.pallas_call(
        cut_kernel,
        in_specs=[pl.BlockSpec(memory_space=pltpu.SMEM), pl.BlockSpec(memory_space=pltpu.HBM)],
        out_specs=[pl.BlockSpec(memory_space=pl.ANY)] * 6,
        out_shape=[jax.ShapeDtypeStruct((HALF, 4, ROWS, N), BF)] * 6,
        scratch_shapes=[
            pltpu.VMEM((6, HALF, 4, ROWS, N), BF),
            pltpu.SemaphoreType.DMA((6,)),
            pltpu.SemaphoreType.DMA((6,)),
        ],
        compiler_params=pltpu.CompilerParams(vmem_limit_bytes=SMALL),
        name="cut",
    )(place, pltpu.with_memory_space_constraint(grads, pltpu.HBM))


def add_kernel(across, place, own, r1, r2, r3, *outs):
    here = place[across]

    @pl.loop(0, HALF)
    def _(b):
        for step, out in enumerate(outs):
            j = lax.rem(here + step, 4)
            out[b] = (own[b, j].astype(F32) + r1[b, j].astype(F32)) + (r2[b, j].astype(F32) + r3[b, j].astype(F32))


def add_pieces(place, pieces, across):
    return pl.pallas_call(
        functools.partial(add_kernel, across),
        in_specs=[pl.BlockSpec(memory_space=pltpu.SMEM)] + [pl.BlockSpec(memory_space=pltpu.VMEM)] * 4,
        out_specs=[pl.BlockSpec(memory_space=pltpu.VMEM)] * 4,
        out_shape=[jax.ShapeDtypeStruct((HALF, ROWS, N), F32)] * 4,
        compiler_params=pltpu.CompilerParams(vmem_limit_bytes=SMALL),
        cost_estimate=pl.CostEstimate(flops=2_000_000, bytes_accessed=4_000_000, transcendentals=0),
    )(place, *pieces)


def add_again_kernel(place, *refs):
    keep, send, total = refs[8], refs[9], refs[10]
    for group in range(2):
        a, b, c, d = (ref[0] for ref in refs[4 * group : 4 * group + 4])
        total[group] = (a + b) + (c + d)
    z = place[2]
    near = pl.multiple_of(z * PIECE, PIECE)
    far = pl.multiple_of((1 - z) * PIECE, PIECE)
    keep[:, 0] = total[:, pl.ds(near, PIECE), :]
    send[:, 0] = total[:, pl.ds(far, PIECE), :]


def add_again(place, first, second):
    spec = pl.BlockSpec((2, 1, PIECE, N), lambda b, p: (0, b, 0, 0))
    return pl.pallas_call(
        add_again_kernel,
        grid_spec=pltpu.PrefetchScalarGridSpec(
            num_scalar_prefetch=1,
            grid=(HALF,),
            in_specs=[pl.BlockSpec((1, ROWS, N), lambda b, p: (b, 0, 0))] * 8,
            out_specs=[spec] * 2,
            scratch_shapes=[pltpu.VMEM((2, ROWS, N), F32)],
        ),
        out_shape=[jax.ShapeDtypeStruct((2, HALF, PIECE, N), F32)] * 2,
        compiler_params=pltpu.CompilerParams(dimension_semantics=("arbitrary",), vmem_limit_bytes=SMALL),
        cost_estimate=pl.CostEstimate(flops=1_000_000, bytes_accessed=3_300_000, transcendentals=0),
        name="add_again",
    )(place, *first, *second)


def pack_kernel(index_ref, keep, recv, out_ref, total, message, sems):
    squares = jnp.zeros((PIECE, N), F32)
    for b in range(BLK):
        value = keep[b // HALF, b % HALF] + recv[b // HALF, b % HALF]
        for c in range(4):
            total[b, pl.ds(c * PIECE, PIECE), :] = value[:, c * 128 : (c + 1) * 128]
        squares += value * value
    square = jnp.broadcast_to(jnp.sum(squares), (8, 128))

    copies = []
    for part in range(4):

        @pl.loop(8 * part, 8 * part + 8)
        def _(o):
            for s in range(SLOTS):
                message[o, pl.ds(s * CHUNK, CHUNK), :] = total[index_ref[s, o]]
            message[o, pl.ds(SLOTS * CHUNK, 8), :] = square

        group = pl.ds(8 * part, 8)
        copies.append(pltpu.make_async_copy(message.at[group], out_ref.at[group], sems.at[part]))
        copies[-1].start()
    for copy in copies:
        copy.wait()


def pack(index, keep, recv):
    return pl.pallas_call(
        pack_kernel,
        in_specs=[pl.BlockSpec(memory_space=pltpu.SMEM)] + [pl.BlockSpec(memory_space=pltpu.VMEM)] * 2,
        out_specs=pl.BlockSpec(memory_space=pl.ANY),
        out_shape=jax.ShapeDtypeStruct((NDP, MESSAGE, 128), F32),
        scratch_shapes=[
            pltpu.VMEM((BLK, CHUNK, 128), F32),
            pltpu.VMEM((NDP, MESSAGE, 128), F32),
            pltpu.SemaphoreType.DMA((4,)),
        ],
        compiler_params=pltpu.CompilerParams(vmem_limit_bytes=SMALL),
        cost_estimate=pl.CostEstimate(flops=300_000, bytes_accessed=3_000_000, transcendentals=0),
        name="pack",
    )(index, keep, recv)


def unpack(full, ref, offset, scale):
    for source in range(NDP):
        for c in range(4):
            piece = ref[source, pl.ds(offset + c * PIECE, PIECE), :]
            full[pl.ds(piece_row(source), PIECE), pl.ds(c * 128, 128)] = piece * scale


def clip_of(sums):
    total = (sums[0][...] + sums[1][...]) + (sums[2][...] + sums[3][...])
    return (1.0 / jnp.sqrt(total / ENTRIES + tiny_offset))[0:1, 0:1]


def piece_row(device):
    return (device % 4) * 128 + (device // 4 % 4) * ROWS + (device // 16) * PIECE


def task_kernel(occ, s0, s1, s2, s3, own_g, own_old, other_g, other_old, own_dir, other_dir, g2, gt2, full, whole, old, norms, sem, *pairs):
    m, f, p, q, m1, f1, x = (pairs[2 * k : 2 * k + 2] for k in range(7))
    task = pl.program_id(0)

    def halves_to(ref):
        return lambda i, j, acc: store_block(ref, i, j, acc)

    def factor(i, j, moving):
        return scaled_eye(1.25) - 0.25 * moving if i == j else -0.25 * moving

    @pl.when(occ[task] > 0)
    def _():
        clip = clip_of((s0, s1, s2, s3))

        @pl.when(task == 0)
        def _():
            pltpu.make_async_copy(other_old.at[0, 0, 0], old, sem).start()
            unpack(full, other_g, 0, clip)

        @pl.when(task == 1)
        def _():
            pltpu.make_async_copy(own_old.at[0, 0, 0], old, sem).start()
            unpack(full, own_g, 0, clip)

        g = full[...]
        squares = jnp.sum(g * g)
        store(g2, pl.ds(0, N), g)
        store(gt2, pl.ds(0, N), g.T)

        def gram(side, a, b):
            def finish(i, j, acc):
                whole[side, *area(i, j)] = (1.0 - decay_rate) * acc + (scaled_eye(ridge_term) if i == j else 0.0)

            symmetric(a, b, finish)

        gram(0, g2, gt2)
        gram(1, gt2, g2)
        pltpu.make_async_copy(own_old.at[0, 0, 0], old, sem).wait()
        sides = (0, 1)
        for side in sides:
            mixed = whole[side] + decay_rate * old[side]
            whole[side] = mixed
            norm2 = jnp.sum(mixed * mixed)
            norms[side] = norm2
            inverse = (1.0 / jnp.sqrt(jnp.full((8, 128), norm2, F32)))[0:1, 0:1]
            for i in range(2):
                for j in range(2):
                    moving = whole[side, *area(i, j)] * inverse
                    store_block(m[side], i, j, moving)
                    store_block(f[side], i, j, factor(i, j, moving))

        def moved(to, factor_to):
            def finish(i, j, acc):
                if to is not None:
                    store_block(to, i, j, acc)
                store_block(factor_to, i, j, factor(i, j, acc))

            return finish

        for side in sides:
            symmetric(f[side], f[side], halves_to(p[side]))
        for side in sides:
            symmetric(p[side], p[side], halves_to(q[side]))
        for side in sides:
            symmetric(q[side], m[side], moved(m1[side], f1[side]))
        for side in sides:
            symmetric(f1[side], f1[side], halves_to(p[side]))
        for side in sides:
            symmetric(f[side], f1[side], halves_to(x[side]))
        for side in sides:
            symmetric(p[side], p[side], halves_to(q[side]))
        for side in sides:
            symmetric(q[side], m1[side], moved(None, m[side]))
        for side in sides:
            symmetric(x[side], m[side], halves_to(f[side]))

        def last(r, rows, acc):
            full[rows, :] = acc

        product(f[0], g2, lambda r, rows, acc: store(p[0], rows, acc))
        product(p[0], f[1], last)
        precond = full[...] * (power_eighth(norms[0]) * power_eighth(norms[1]))
        entries = N * N
        actual = jnp.full((8, 128), jnp.sum(precond * precond) / entries + tiny_offset, F32)
        target = jnp.full((8, 128), squares / entries + tiny_offset, F32)
        graft = (jnp.sqrt(target) / jnp.sqrt(actual))[0:1, 0:1]
        full[...] = precond * graft

        @pl.when(task == 0)
        def _():
            for device in range(NDP):
                other_dir[device, 0] = full[pl.ds(piece_row(device), PIECE), :].astype(BF)

        @pl.when(task == 1)
        def _():
            for device in range(NDP):
                own_dir[device, 0] = full[pl.ds(piece_row(device), PIECE), :].astype(BF)


def pair():
    return pltpu.VMEM((2, N, N), BF)


def run_tasks(occupied, sums, own_g, own_pairs, other_g, other_pair):
    result = jax.ShapeDtypeStruct((NDP, 1, PIECE, N), BF)
    return pl.pallas_call(
        task_kernel,
        grid=(2,),
        in_specs=[pl.BlockSpec(memory_space=pltpu.SMEM)]
        + [pl.BlockSpec(memory_space=pltpu.VMEM)] * 4
        + [pl.BlockSpec(memory_space=space) for space in (pltpu.VMEM, pltpu.HBM, pltpu.VMEM, pltpu.HBM)],
        out_specs=[pl.BlockSpec(memory_space=pltpu.VMEM)] * 2,
        out_shape=[result, result],
        scratch_shapes=[pair(), pair(), pltpu.VMEM((N, N), F32)]
        + [pltpu.VMEM((2, N, N), F32), pltpu.VMEM((2, N, N), F32), pltpu.SMEM((2,), F32), pltpu.SemaphoreType.DMA]
        + [pair() for _ in range(14)],
        compiler_params=pltpu.CompilerParams(dimension_semantics=("arbitrary",), vmem_limit_bytes=36 << 20),
        cost_estimate=pl.CostEstimate(flops=16_000_000_000, bytes_accessed=3_500_000, transcendentals=0),
        name="tasks",
    )(occupied, *sums, own_g, pltpu.with_memory_space_constraint(own_pairs, pltpu.HBM), other_g, other_pair)


def state_kernel(occ, s0, s1, s2, s3, g_ref, old_ref, new_ref, full, g2, gt2):
    s = pl.program_id(0)

    @pl.when(occ[s] > 0)
    def _():
        unpack(full, g_ref, pl.multiple_of(s * CHUNK, CHUNK), clip_of((s0, s1, s2, s3)))
        g = full[...]
        store(g2, pl.ds(0, N), g)
        store(gt2, pl.ds(0, N), g.T)

        def mix(side):
            def finish(r, rows, acc):
                new_ref[0, 0, 0, side, rows, :] = (
                    decay_rate * old_ref[0, 0, 0, side, rows, :] + (1.0 - decay_rate) * acc
                )

            return finish

        product(g2, gt2, mix(0))
        product(gt2, g2, mix(1))

    @pl.when(occ[s] <= 0)
    def _():
        new_ref[...] = old_ref[...]


def new_state(occupied, sums, gathered, pairs):
    block = pl.BlockSpec((1, 1, 1, 2, N, N), lambda s: (0, 0, s, 0, 0, 0))
    return pl.pallas_call(
        state_kernel,
        grid=(SLOTS,),
        in_specs=[
            pl.BlockSpec(memory_space=pltpu.SMEM),
        ]
        + [pl.BlockSpec(memory_space=pltpu.VMEM)] * 5
        + [block],
        out_specs=block,
        out_shape=jax.ShapeDtypeStruct(pairs.shape, F32),
        scratch_shapes=[pltpu.VMEM((N, N), F32), pair(), pair()],
        compiler_params=pltpu.CompilerParams(dimension_semantics=("arbitrary",), vmem_limit_bytes=SMALL),
        cost_estimate=pl.CostEstimate(flops=3_000_000_000, bytes_accessed=10_000_000, transcendentals=0),
        name="state",
    )(occupied, *sums, gathered, pairs)


def pick_kernel(owner, slot, recv_ref, out_ref):
    for b in range(BLK):
        out_ref[b] = recv_ref[owner[b], slot[b]]


def pick(owner, slot, recv):
    return pl.pallas_call(
        pick_kernel,
        in_specs=[pl.BlockSpec(memory_space=pltpu.SMEM)] * 2 + [pl.BlockSpec(memory_space=pltpu.VMEM)],
        out_specs=pl.BlockSpec(memory_space=pltpu.VMEM),
        out_shape=jax.ShapeDtypeStruct((BLK, PIECE, N), BF),
        compiler_params=pltpu.CompilerParams(vmem_limit_bytes=SMALL),
        name="pick",
    )(owner, slot, recv)


def place_kernel(steps, place, *refs):
    count = 2 * len(steps)
    groups, out, sems = (refs[: len(steps)], refs[len(steps) : count]), refs[-2], refs[-1]
    x, y, z = place[0], place[1], place[2]
    copies = []
    for number, (far, low) in enumerate(steps):
        for near in range(2) if far == 2 else range(4):
            for dz in range(2):
                for group in range(2):
                    dx, dy = (far, near + low) if group == 0 else (near + low, far)
                    row = lax.rem(z + dz, 2) * PIECE + lax.rem(y + 4 - dy, 4) * ROWS + lax.rem(x + 4 - dx, 4) * 128
                    copies.append(
                        pltpu.make_async_copy(
                            groups[group][number].at[near, dz],
                            out.at[pl.ds(group * HALF, HALF), pl.ds(pl.multiple_of(row, PIECE), PIECE), :],
                            sems.at[len(copies)],
                        )
                    )
    for copy in copies:
        copy.start()
    for copy in copies:
        copy.wait()


def place_some(place, first, second, steps, placed):
    refs = [*first, *second] + ([] if placed is None else [placed])
    return pl.pallas_call(
        functools.partial(place_kernel, steps),
        in_specs=[pl.BlockSpec(memory_space=pltpu.SMEM)]
        + [pl.BlockSpec(memory_space=pltpu.VMEM)] * (2 * len(steps))
        + ([] if placed is None else [pl.BlockSpec(memory_space=pl.ANY)]),
        out_specs=pl.BlockSpec(memory_space=pl.ANY),
        out_shape=jax.ShapeDtypeStruct((BLK, N, N), BF),
        scratch_shapes=[pltpu.SemaphoreType.DMA((48 if placed is None else 16,))],
        input_output_aliases={} if placed is None else {len(refs): 0},
        compiler_params=pltpu.CompilerParams(vmem_limit_bytes=SMALL),
        cost_estimate=pl.CostEstimate(flops=0, bytes_accessed=8_000_000, transcendentals=0),
        name="place" if placed is None else "place_last",
    )(place, *refs)


def place_all(place, first, second):
    near = place_some(place, first[:3], second[:3], ((0, 0), (1, 0), (3, 0)), None)
    return place_some(place, first[3:], second[3:], ((2, 0), (2, 2)), near)


def spread(v, dx, dy, dz):
    steps = 2 if dz else 4
    return [v] + [lax.ppermute(v, "dp", dp_pairs(dx * k, dy * k, dz * k)) for k in range(1, steps)]


def around(v, dx, dy):
    ahead, behind = dp_pairs(dx, dy, 0), dp_pairs(3 * dx, 3 * dy, 0)
    back = lax.ppermute(v, "dp", ahead)
    front = lax.ppermute(v, "dp", behind)
    return [v, back, front, lax.ppermute(back[:2], "dp", ahead), lax.ppermute(front[2:], "dp", behind)]


def spread(v, dx, dy, dz):
    steps = 2 if dz else 4
    return [v] + [lax.ppermute(v, "dp", dp_pairs(dx * k, dy * k, dz * k)) for k in range(1, steps)]


def owner_slots(owners):
    positions = jnp.arange(owners.shape[0], dtype=jnp.int32)
    same_owner = owners[:, None] == owners[None, :]
    earlier = positions[None, :] < positions[:, None]
    return jnp.sum((same_owner & earlier).astype(jnp.int32), axis=1)


def shards(gradients, factor_state, block_owner):
    owners = block_owner[0]
    myself = lax.axis_index("dp")
    slot_of = owner_slots(owners)
    positions = jnp.arange(BLK, dtype=jnp.int32)
    slots = jnp.arange(SLOTS, dtype=jnp.int32)
    devices = jnp.arange(NDP, dtype=jnp.int32)
    match = (owners == devices[None, :, None]) & (slot_of == slots[:, None, None])
    index = jnp.sum(jnp.where(match, positions, 0), axis=2)
    mine = (owners == myself) & (slot_of == slots[:, None])
    occupied = jnp.max(mine.astype(jnp.int32), axis=1)
    other_occupied = lax.ppermute(occupied[1:2], "mp", CORE_PAIRS)
    other_pair = lax.ppermute(factor_state[:, :, 1:2], "mp", CORE_PAIRS)

    place = jnp.stack([myself % 4, (myself // 4) % 4, myself // 16]).astype(jnp.int32)
    grads = gradients[0].reshape(BLK, 4, 4, ROWS, N)
    pieces = cut(place, grads)
    grads, pieces = lax.optimization_barrier((grads, pieces))
    first, second = [None] * 4, [None] * 4
    for k in (1, 3, 2):
        first[k] = lax.ppermute(pieces[k - 1], "dp", dp_pairs(k, 0, 0))
        second[k] = lax.ppermute(pieces[k + 2], "dp", dp_pairs(0, k, 0))
    zero = jnp.int32(0)
    start = (zero, place[0], zero, zero, zero)
    first[0] = lax.dynamic_slice(grads, start, (HALF, 1, 4, ROWS, N)).reshape(HALF, 4, ROWS, N)
    start = (jnp.int32(HALF), zero, place[1], zero, zero)
    second[0] = lax.dynamic_slice(grads, start, (HALF, 4, 1, ROWS, N)).reshape(HALF, 4, ROWS, N)
    tasks = jnp.concatenate([other_occupied, occupied[0:1]])
    first[0], index, tasks, occupied = lax.optimization_barrier((first[0], index, tasks, occupied))
    first = list(add_pieces(place, first, 1))
    second = list(add_pieces(place, second, 0))
    for k in (1, 3, 2):
        first[k] = lax.ppermute(first[k], "dp", dp_pairs(0, k, 0))
        second[k] = lax.ppermute(second[k], "dp", dp_pairs(k, 0, 0))
    keep, send = add_again(place, first, second)
    packed = pack(index, keep, lax.ppermute(send, "dp", dp_pairs(0, 0, 1)))
    gathered = lax.all_to_all(packed, "dp", split_axis=0, concat_axis=0, tiled=True)
    other = lax.ppermute(gathered[:, CHUNK : 2 * CHUNK], "mp", CORE_PAIRS)
    squares = jnp.sum(gathered[:, SLOTS * CHUNK :], axis=0)
    sums = [squares] + [lax.ppermute(squares, "mp", [(i, i ^ bit) for i in range(4)]) for bit in (1, 2, 3)]
    own, helped = run_tasks(tasks, sums, gathered, factor_state, other, other_pair)
    returned = lax.ppermute(helped, "mp", CORE_PAIRS)
    outgoing = jnp.concatenate([own, returned], axis=1)
    incoming = lax.all_to_all(outgoing, "dp", split_axis=0, concat_axis=0, tiled=True)
    piece = pick(owners, slot_of, incoming)

    column = jnp.stack(spread(piece, 0, 0, 1))
    first = jnp.stack(spread(column[:, :HALF], 0, 1, 0))
    second = jnp.stack(spread(column[:, HALF:], 1, 0, 0))
    first = around(first, 1, 0)
    second = around(second, 0, 1)
    directions = place_all(place, first, second)
    next_state = new_state(occupied, sums, gathered, factor_state)
    return directions, next_state


def solution(mesh):
    in_specs = (P("dp", "mp", None, None), P("mp", "dp", None, None, None, None), P("mp", None))
    out_specs = (P("mp", None, None), P("mp", "dp", None, None, None, None))
    return jax.shard_map(shards, mesh=mesh, in_specs=in_specs, out_specs=out_specs, check_vma=False)
```
